32 devices in a mesh: row: 4 (over z), col: 4 (over x, core), grid: 2 (over y).
Axes of the slice: x: 2, y: 2, z: 4, core: 2. Of those that a mesh axis runs over, the one named last changes fastest.
Arguments:
- tokens: bfloat16 [2, 4096, 2048], P(None, ('row', 'col'), 'grid'), may hold values from -6 to 6
- cotangent: bfloat16 [2, 4096, 2048], P(None, ('row', 'col'), 'grid'), may hold values from -6 to 6
- lengths: int32 [2, 4, 2, 4], replicated, may hold values from 0 to 512, as said below
- deal_pages: int32 [2, 4, 4, 4], replicated, may hold values from 0 to 3, each once within a row
- land_slots: int32 [2, 4, 4, 4], replicated, may hold values from 0 to 3, each once within a row
- pre_gain: float32 [2048], P('grid'), may hold values from 0.5 to 1.5
- pre_bias: float32 [2048], P('grid'), may hold values from -2.5 to 2.5
- query_weight: bfloat16 [2048, 2048], P('grid', 'col'), may hold values from -0.088388348 to 0.088388348
- key_weight: bfloat16 [2048, 2048], P('grid', 'col'), may hold values from -0.088388348 to 0.088388348
- value_weight: bfloat16 [2048, 4096], P('grid', 'col'), may hold values from -0.125 to 0.125
- gate_weight: bfloat16 [2048, 4096], P('grid', 'col'), may hold values from -0.125 to 0.125
- group_gain: float32 [4096], P('col'), may hold values from 0.5 to 1.5
- group_bias: float32 [4096], P('col'), may hold values from -2.5 to 2.5
- output_weight: bfloat16 [4096, 2048], P('col', 'grid'), may hold values from -0.125 to 0.125
- mid_gain: float32 [2048], P('grid'), may hold values from 0.5 to 1.5
- mid_bias: float32 [2048], P('grid'), may hold values from -2.5 to 2.5
- up_weight: bfloat16 [2048, 4096], P('grid', 'col'), may hold values from -0.125 to 0.125
- down_weight: bfloat16 [4096, 2048], P('col', 'grid'), may hold values from -0.125 to 0.125
Outputs:
- block_out: bfloat16 [2, 4096, 2048], P(None, ('row', 'col'), 'grid')
- tokens_grad: bfloat16 [2, 4096, 2048], P(None, ('row', 'col'), 'grid')
- pregain_grad: float32 [2048], P('grid')
- prebias_grad: float32 [2048], P('grid')
- query_grad: float32 [2048, 2048], P('grid', 'col')
- key_grad: float32 [2048, 2048], P('grid', 'col')
- value_grad: float32 [2048, 4096], P('grid', 'col')
- gating_grad: float32 [2048, 4096], P('grid', 'col')
- groupgain_grad: float32 [4096], P('col')
- groupbias_grad: float32 [4096], P('col')
- output_grad: float32 [4096, 2048], P('col', 'grid')
- midgain_grad: float32 [2048], P('grid')
- midbias_grad: float32 [2048], P('grid')
- upward_grad: float32 [2048, 4096], P('grid', 'col')
- downward_grad: float32 [4096, 2048], P('col', 'grid')
The draws below stay inside these ranges and needn't reach their ends.
Inputs may be any that keep to these rules, and one draw needn't show every extreme that they name: The 4 lengths of a cell sum to 512; a length may be 0; in every micro-batch the cell of row 0 and grid index 0 holds one sequence of 512 tokens. For every micro-batch, column and source row, deal_pages is a permutation of the pages. For every micro-batch, column and destination row, land_slots is a permutation of the slots.
All inputs are finite; a program needn't handle non-finite values.
Results may differ from the reference program's by a relative error of at most 0.018.
Values may be sent and summed in bfloat16 or wider, within the bound.
No kernel may reach another device: no remote copies, remote signals or barrier semaphores. Data moves between devices by JAX's collectives and lax.ppermute only.
A program may use at most 256 MiB of HBM per device.

```python
import jax
import jax.numpy as jnp
from jax import lax

D = 2048
HEADS = 8
QK_HEAD = 256
V_HEAD = 512
FF = 4096
QKD = 2048
VD = 4096
TD = 256
MB = 2
CH = 512
SEGS = 4
PAGE = 64
CELL = 512
TOKENS_MB = 4096
N_ROW = 4
N_COL = 4
N_GRID = 2


def draw_lengths(key, part):
    cuts = jax.random.randint(key, (MB, N_ROW, N_GRID, SEGS - 1), 0, CELL + 1)
    cuts = jnp.sort(cuts, axis=-1)
    lower = jnp.zeros((MB, N_ROW, N_GRID, 1), jnp.int32)
    upper = jnp.full((MB, N_ROW, N_GRID, 1), CELL, jnp.int32)
    edges = jnp.concatenate([lower, cuts.astype(jnp.int32), upper], axis=-1)
    lens = edges[..., 1:] - edges[..., :-1]
    single = jnp.zeros((SEGS,), jnp.int32).at[0].set(CELL)
    lens = lens.at[:, 0, 0, :].set(single)
    return lens.astype(jnp.int32)


def shared_projections(key):
    common = jax.random.truncated_normal(jax.random.fold_in(key, 7001), -4.0, 4.0, (D, QKD), jnp.float32)
    own = jax.random.truncated_normal(jax.random.fold_in(key, 7002), -4.0, 4.0, (D, QKD), jnp.float32)
    scale = D ** (-0.5)
    query_part = common * scale
    key_part = jnp.clip(0.8 * common + 0.6 * own, -4.0, 4.0) * scale
    return (query_part, key_part)


def draw_query_weight(key, part):
    return shared_projections(key)[0].astype(jnp.bfloat16)


def draw_key_weight(key, part):
    return shared_projections(key)[1].astype(jnp.bfloat16)


def block_levels(key, extent, cuts, least, largest):
    level, own = 1.0, jax.random.fold_in(key, 6)
    for position, parts in cuts:
        draws = jnp.exp(jax.random.uniform(jax.random.fold_in(own, position), (parts,), jnp.float32, least / len(cuts), largest / len(cuts)))
        level = level * jnp.repeat(draws, extent[position] // parts).reshape([-1 if axis == position else 1 for axis in range(len(extent))])
    return level


def gaussian(stream_key, dims, deviation, limit, shards=(), kind=jnp.bfloat16):
    factor_of = block_levels(stream_key, dims, shards, -0.22, 0.18) if shards else 1.0
    values = jax.random.normal(stream_key, dims, jnp.float32) * deviation * factor_of
    return jnp.minimum(jnp.maximum(values, -limit), limit).astype(kind)


def setup_inputs(seed: int = 0) -> dict:
    streams_of = jax.random.split(jax.random.key(seed), 19)
    return {
        "tokens": gaussian(streams_of[0], (MB, TOKENS_MB, D), 1.0, 6.0, ((1, 16), (2, 2))),
        "cotangent": gaussian(streams_of[1], (MB, TOKENS_MB, D), 1.0, 6.0, ((1, 16), (2, 2))),
        "lengths": draw_lengths(jax.random.fold_in(streams_of[18], 71), 0),
        "deal_pages": jax.vmap(lambda own: jax.random.permutation(own, N_ROW))(jax.random.split(streams_of[3], MB * N_COL * N_ROW)).reshape((MB, N_COL, N_ROW, N_ROW)).astype(jnp.int32),
        "land_slots": jax.vmap(lambda own: jax.random.permutation(own, N_ROW))(jax.random.split(streams_of[4], MB * N_COL * N_ROW)).reshape((MB, N_COL, N_ROW, N_ROW)).astype(jnp.int32),
        "pre_gain": jnp.clip(1.0 + 0.1 * jax.random.normal(streams_of[5], (D,), jnp.float32), 0.5, 1.5),
        "pre_bias": gaussian(streams_of[6], (D,), 0.3, 2.5, ((0, 2),), jnp.float32),
        "query_weight": draw_query_weight(jax.random.fold_in(streams_of[18], 71), 0),
        "key_weight": draw_key_weight(jax.random.fold_in(streams_of[18], 71), 0),
        "value_weight": gaussian(streams_of[9], (D, VD), D ** -0.5, 0.125, ((0, 2), (1, 4))),
        "gate_weight": gaussian(streams_of[10], (D, VD), D ** -0.5, 0.125, ((0, 2), (1, 4))),
        "group_gain": jnp.clip(1.0 + 0.1 * jax.random.normal(streams_of[11], (VD,), jnp.float32), 0.5, 1.5),
        "group_bias": gaussian(streams_of[12], (VD,), 0.3, 2.5, ((0, 4),), jnp.float32),
        "output_weight": gaussian(streams_of[13], (VD, D), (VD // 2) ** -0.5, 0.125, ((0, 4), (1, 2))),
        "mid_gain": jnp.clip(1.0 + 0.1 * jax.random.normal(streams_of[14], (D,), jnp.float32), 0.5, 1.5),
        "mid_bias": gaussian(streams_of[15], (D,), 0.3, 2.5, ((0, 2),), jnp.float32),
        "up_weight": gaussian(streams_of[16], (D, FF), D ** -0.5, 0.125, ((0, 2), (1, 4))),
        "down_weight": gaussian(streams_of[17], (FF, D), (FF // 2) ** -0.5, 0.125, ((0, 4), (1, 2))),
    }


epsilon = 1e-05
highest = lax.Precision.HIGHEST

@jax.custom_vjp
def low(v):
    return lax.optimization_barrier(v.astype(jnp.bfloat16)).astype(jnp.float32)

@jax.custom_vjp
def low_back(v):
    return v

def low_keep(v):
    return (low(v), None)

def low_pass(kept, grad):
    return (grad,)

def back_keep(v):
    return (v, None)

def back_low(kept, grad):
    return (low(grad),)
low.defvjp(low_keep, low_pass)
low_back.defvjp(back_keep, back_low)

def matmul(left, right):
    return jnp.dot(left, right, preferred_element_type=jnp.float32, precision=highest)

def layer_norm(values, gain, bias):
    centre = lax.optimization_barrier(jnp.mean(values, axis=-1, keepdims=True))
    variance = lax.optimization_barrier(jnp.mean(values * values, axis=-1, keepdims=True)) - centre * centre
    return (values - centre) * lax.rsqrt(variance + epsilon) * gain + bias

def turn(values):
    half = values.shape[-1] // 2
    return jnp.concatenate([-values[..., half:], values[..., :half]], axis=-1)

def rotary_tables(count):
    positions = (jnp.arange(count, dtype=jnp.int32) % CELL).astype(jnp.float32)
    rates = 10000.0 ** (-jnp.arange(QK_HEAD // 2, dtype=jnp.int32).astype(jnp.float32) / (QK_HEAD // 2))
    angles = positions[:, None] * rates[None, :]
    angles = jnp.concatenate([angles, angles], axis=1)[:, None, :]
    return (jnp.cos(angles), jnp.sin(angles))

def log_rates():
    return jnp.log1p(-jnp.exp2(-5.0 - jnp.arange(HEADS, dtype=jnp.int32).astype(jnp.float32)))

def block_masks(segment, previous, log_decay, block):
    place = jnp.arange(block, dtype=jnp.int32)
    distance = place[:, None] - place[None, :]
    same = (segment[:, None] == segment[None, :]) & (distance >= 0)
    zero = jnp.zeros((), log_decay.dtype)
    decay = jnp.where(same[None], jnp.exp(log_decay[:, None, None] * jnp.maximum(distance, 0)[None].astype(log_decay.dtype)), zero)
    cross = jnp.where((segment == previous)[None, :], jnp.exp(log_decay[:, None] * (place + 1)[None].astype(log_decay.dtype)), zero)
    last = segment[block - 1].astype(jnp.int32)
    keep = jnp.where((segment == last)[None, :], jnp.exp(log_decay[:, None] * (block - 1 - place)[None].astype(log_decay.dtype)), zero)
    carry_weight = jnp.where(last == previous, jnp.exp(log_decay * block), zero)
    return (decay, cross, keep, carry_weight, last)

def retention_block(carry, pieces):
    state, previous = carry
    query, keys, values, segment = pieces
    decay, cross, keep, carry_weight, last = block_masks(segment, previous, log_rates().astype(state.dtype), CH)
    scale = QK_HEAD ** (-0.5)
    raw = jnp.einsum('ihd,jhd->hij', query, keys, precision=highest)
    weights = low(low_back(raw) * scale * decay)
    inner = jnp.einsum('hij,jhe->ihe', weights, values, precision=highest)
    scaled = low(query * (cross.T[:, :, None] * scale))
    outer = jnp.einsum('ihd,hde->ihe', scaled, low(state), precision=highest)
    kept = low(keys * keep.T[:, :, None])
    added = jnp.einsum('jhd,jhe->hde', kept, values, precision=highest)
    new_state = (carry_weight[:, None, None] * state + low_back(added)).astype(state.dtype)
    return ((new_state, last), (inner + outer).astype(state.dtype))

def cell_retention(pieces):
    query, keys, values, lens = pieces
    ends = jnp.cumsum(lens).astype(jnp.int32)
    place = jnp.arange(CELL, dtype=jnp.int32)
    segment = lax.optimization_barrier(jnp.sum((place[:, None] >= ends[None, :]).astype(jnp.int32), axis=1)).astype(jnp.int32)
    blocks = CELL // CH
    split = (query.reshape(blocks, CH, HEADS, QK_HEAD), keys.reshape(blocks, CH, HEADS, QK_HEAD), values.reshape(blocks, CH, HEADS, V_HEAD), segment.reshape(blocks, CH))
    start = (jnp.zeros((HEADS, QK_HEAD, V_HEAD), query.dtype), jnp.array(-1, jnp.int32))
    _, outputs = lax.scan(jax.checkpoint(retention_block), start, split)
    return outputs.reshape(CELL, HEADS, V_HEAD)

def forward(inputs, lens, params):
    pre_gain, pre_bias, query_weight, key_weight, value_weight, gate_weight, group_gain, group_bias, output_weight, mid_gain, mid_bias, up_weight, down_weight = params
    count = inputs.shape[0]
    hidden_one = low(layer_norm(inputs, pre_gain, pre_bias))
    query = low_back(matmul(hidden_one, query_weight)).reshape(count, HEADS, QK_HEAD)
    keys = low_back(matmul(hidden_one, key_weight)).reshape(count, HEADS, QK_HEAD)
    values = low_back(matmul(hidden_one, value_weight))
    gate = low_back(matmul(hidden_one, gate_weight))
    cosines, sines = rotary_tables(count)
    cosines = cosines.astype(query.dtype)
    sines = sines.astype(query.dtype)
    query_low = low(query * cosines + turn(query) * sines)
    key_low = low(keys * cosines + turn(keys) * sines)
    value_low = low(values).reshape(count, HEADS, V_HEAD)
    cells = count // CELL
    mixed = lax.map(cell_retention, (query_low.reshape(cells, CELL, HEADS, QK_HEAD), key_low.reshape(cells, CELL, HEADS, QK_HEAD), value_low.reshape(cells, CELL, HEADS, V_HEAD), lens.astype(jnp.int32)))
    mixed = low_back(mixed.reshape(count, HEADS, V_HEAD))
    centre = lax.optimization_barrier(jnp.mean(mixed, axis=-1, keepdims=True))
    centered = mixed - centre
    variance = lax.optimization_barrier(jnp.mean(centered * centered, axis=-1, keepdims=True))
    normed = (centered * lax.rsqrt(variance + epsilon)).reshape(count, VD) * group_gain + group_bias
    gated = low(jax.nn.silu(gate) * normed)
    resid = inputs + low_back(matmul(gated, output_weight))
    hidden_two = low(layer_norm(resid, mid_gain, mid_bias))
    pre_act = low_back(matmul(hidden_two, up_weight))
    activated = low(jax.nn.gelu(pre_act, approximate=False))
    return resid + low_back(matmul(activated, down_weight))

def source_index(deal_pages, land_slots):
    ranks = jnp.arange(N_ROW, dtype=jnp.int32)
    from_row = lax.optimization_barrier(jnp.sum(ranks * (land_slots[..., None, :] == ranks[:, None]).astype(jnp.int32), axis=-1)).astype(jnp.int32)
    dealt = jnp.swapaxes(deal_pages, 2, 3).astype(jnp.int32)
    from_page = jnp.take_along_axis(dealt, from_row, axis=3).astype(jnp.int32)
    columns = jnp.arange(N_COL, dtype=jnp.int32)[None, :, None, None]
    start = (from_row * N_COL + columns) * TD + from_page * PAGE
    start = jnp.transpose(start, (0, 2, 1, 3)).astype(jnp.int32)
    inner = jnp.arange(PAGE, dtype=jnp.int32)
    return (start[..., None] + inner).reshape(MB, TOKENS_MB).astype(jnp.int32)

def reference(tokens, cotangent, lengths, deal_pages, land_slots, pre_gain, pre_bias, query_weight, key_weight, value_weight, gate_weight, group_gain, group_bias, output_weight, mid_gain, mid_bias, up_weight, down_weight):
    index = source_index(deal_pages, land_slots)
    take = jax.vmap(lambda source, order: source[order])
    inputs = take(tokens, index).astype(jnp.float32)
    grads_in = take(cotangent, index).astype(jnp.float32)
    params = tuple((weight.astype(jnp.float32) for weight in (pre_gain, pre_bias, query_weight, key_weight, value_weight, gate_weight, group_gain, group_bias, output_weight, mid_gain, mid_bias, up_weight, down_weight)))
    lens = lengths.reshape(MB, N_ROW * N_GRID, SEGS).astype(jnp.int32)

    def batch_step(totals, batch):
        batch_in, batch_grad, batch_lens = batch
        result, pull = jax.vjp(lambda first, *rest: forward(first, batch_lens, rest), batch_in, *params)
        grads = pull(batch_grad)
        totals = tuple(((total + grad).astype(total.dtype) for total, grad in zip(totals, grads[1:])))
        return (totals, (result.astype(batch_in.dtype), grads[0].astype(batch_in.dtype)))
    zeros = tuple((jnp.zeros(weight.shape, weight.dtype) for weight in params))
    totals, (results, input_grads) = lax.scan(batch_step, zeros, (inputs, grads_in, lens))
    restore = jax.vmap(lambda source, order: jnp.zeros_like(source).at[order].set(source))
    block_out = restore(results, index).astype(jnp.bfloat16)
    tokens_grad = restore(input_grads, index).astype(jnp.bfloat16)
    return (block_out, tokens_grad, totals[0], totals[1], totals[2], totals[3], totals[4], totals[5], totals[6], totals[7], totals[8], totals[9], totals[10], totals[11], totals[12])
```

```python
import jax
import jax.numpy as jnp
from jax import lax
from jax.sharding import PartitionSpec as P

D = 2048
QK_HEAD = 256
V_HEAD = 512
CH = 512


epsilon = 1e-05


def shortened(array):

    def short(part):
        return part.astype(jnp.bfloat16) if part.dtype == jnp.float32 else part

    return jax.tree.map(short, array)


def turn(values):
    half = values.shape[-1] // 2
    return jnp.concatenate([-values[..., half:], values[..., :half]], axis=-1)


def turn_back(values):
    half = values.shape[-1] // 2
    return jnp.concatenate([values[..., half:], -values[..., :half]], axis=-1)


def rotary_tables(length, width):
    positions = jnp.arange(length, dtype=jnp.int32).astype(jnp.float32)
    rates = 10000.0 ** (-jnp.arange(width // 2).astype(jnp.float32) / (width // 2))
    angles = positions[:, None] * rates[None, :]
    angles = jnp.concatenate([angles, angles], axis=1)[:, None, :]
    return (jnp.cos(angles), jnp.sin(angles))


def block_masks(segment, previous, log_decay, block):
    place = jnp.arange(block, dtype=jnp.int32)
    distance = place[:, None] - place[None, :]
    same = (segment[:, None] == segment[None, :]) & (distance >= 0)
    decay = jnp.where(
        same[None],
        jnp.exp(log_decay[:, None, None] * jnp.maximum(distance, 0)[None].astype(jnp.float32)),
        0.0,
    )
    cross = jnp.where(
        (segment == previous)[None, :],
        jnp.exp(log_decay[:, None] * (place + 1)[None].astype(jnp.float32)),
        0.0,
    )
    last = segment[block - 1]
    keep = jnp.where(
        (segment == last)[None, :],
        jnp.exp(log_decay[:, None] * (block - 1 - place)[None].astype(jnp.float32)),
        0.0,
    )
    carry_weight = jnp.where(last == previous, jnp.exp(log_decay * block), 0.0)
    return (decay, cross, keep, carry_weight, last)


def retention_forward(query, keys, values, segment, log_decay, block):
    length, heads, width = query.shape
    blocks = length // block
    scale = width ** (-0.5)
    split = (
        query.reshape(blocks, block, heads, width),
        keys.reshape(blocks, block, heads, width),
        values.reshape(blocks, block, heads, values.shape[2]),
        segment.reshape(blocks, block),
    )

    def advance(carry, pieces):
        state, previous = carry
        query_b, keys_b, values_b, segment_b = pieces
        decay, cross, keep, carry_weight, last = block_masks(segment_b, previous, log_decay, block)
        raw = jnp.einsum("ihd,jhd->hij", query_b, keys_b, preferred_element_type=jnp.float32)
        weights = (raw * scale * decay).astype(jnp.bfloat16)
        inner = jnp.einsum("hij,jhe->ihe", weights, values_b, preferred_element_type=jnp.float32)
        scaled = (query_b.astype(jnp.float32) * (cross.T[:, :, None] * scale)).astype(jnp.bfloat16)
        outer = jnp.einsum(
            "ihd,hde->ihe", scaled, state.astype(jnp.bfloat16), preferred_element_type=jnp.float32
        )
        kept = (keys_b.astype(jnp.float32) * keep.T[:, :, None]).astype(jnp.bfloat16)
        added = jnp.einsum("jhd,jhe->hde", kept, values_b, preferred_element_type=jnp.float32)
        new_state = carry_weight[:, None, None] * state + added
        return ((new_state, last), (inner + outer, state))

    start = (jnp.zeros((heads, width, values.shape[2]), jnp.float32), jnp.array(-1, jnp.int32))
    _, (outputs, states) = lax.scan(advance, start, split)
    return (outputs.reshape(length, heads, values.shape[2]), states)


def retention_backward(query, keys, values, segment, states, grad_out, log_decay, block):
    length, heads, width = query.shape
    vwidth = values.shape[2]
    blocks = length // block
    scale = width ** (-0.5)
    segment_blocks = segment.reshape(blocks, block)
    previous_all = jnp.concatenate([jnp.full((1,), -1, jnp.int32), segment_blocks[:-1, -1]])
    split = (
        query.reshape(blocks, block, heads, width),
        keys.reshape(blocks, block, heads, width),
        values.reshape(blocks, block, heads, vwidth),
        segment_blocks,
        previous_all,
        states,
        grad_out.reshape(blocks, block, heads, vwidth),
    )

    def retreat(grad_state, pieces):
        query_b, keys_b, values_b, segment_b, previous, state, grad_b = pieces
        decay, cross, keep, carry_weight, last = block_masks(segment_b, previous, log_decay, block)
        raw = jnp.einsum("ihd,jhd->hij", query_b, keys_b, preferred_element_type=jnp.float32)
        weights = (raw * scale * decay).astype(jnp.bfloat16)
        grad_weights = jnp.einsum(
            "ihe,jhe->hij", grad_b, values_b, preferred_element_type=jnp.float32
        )
        grad_raw = (grad_weights * decay * scale).astype(jnp.bfloat16)
        grad_query = jnp.einsum(
            "hij,jhd->ihd", grad_raw, keys_b, preferred_element_type=jnp.float32
        )
        grad_keys = jnp.einsum(
            "hij,ihd->jhd", grad_raw, query_b, preferred_element_type=jnp.float32
        )
        grad_values = jnp.einsum(
            "hij,ihe->jhe", weights, grad_b, preferred_element_type=jnp.float32
        )
        scaled = (query_b.astype(jnp.float32) * (cross.T[:, :, None] * scale)).astype(jnp.bfloat16)
        grad_scaled = jnp.einsum(
            "ihe,hde->ihd", grad_b, state.astype(jnp.bfloat16), preferred_element_type=jnp.float32
        )
        grad_query = grad_query + grad_scaled * (cross.T[:, :, None] * scale)
        grad_state_low = jnp.einsum(
            "ihd,ihe->hde", scaled, grad_b, preferred_element_type=jnp.float32
        )
        grad_added = grad_state.astype(jnp.bfloat16)
        kept = (keys_b.astype(jnp.float32) * keep.T[:, :, None]).astype(jnp.bfloat16)
        grad_kept = jnp.einsum(
            "jhe,hde->jhd", values_b, grad_added, preferred_element_type=jnp.float32
        )
        grad_keys = grad_keys + grad_kept * keep.T[:, :, None]
        grad_values = grad_values + jnp.einsum(
            "jhd,hde->jhe", kept, grad_added, preferred_element_type=jnp.float32
        )
        new_grad = carry_weight[:, None, None] * grad_state + grad_state_low
        return (new_grad, (grad_query, grad_keys, grad_values))

    start = jnp.zeros((heads, width, vwidth), jnp.float32)
    _, (grad_query, grad_keys, grad_values) = lax.scan(retreat, start, split, reverse=True)
    return (
        grad_query.reshape(length, heads, width),
        grad_keys.reshape(length, heads, width),
        grad_values.reshape(length, heads, vwidth),
    )


def feature_sums(first, second):
    return lax.psum((first, second), "grid")


def layer_stats_norm(values, gain, bias):
    first, second = feature_sums(jnp.sum(values, axis=1), jnp.sum(values * values, axis=1))
    centre = first / D
    spread = lax.rsqrt(second / D - centre * centre + epsilon)
    normal = (values - centre[:, None]) * spread[:, None]
    return (normal * gain + bias, normal, spread)


def norm_back(grad, normal, spread, gain):
    scaled = grad * gain
    first, second = feature_sums(jnp.sum(scaled, axis=1), jnp.sum(scaled * normal, axis=1))
    back = (scaled - first[:, None] / D - normal * (second[:, None] / D)) * spread[:, None]
    return (back, jnp.sum(grad * normal, axis=0), jnp.sum(grad, axis=0))


def project_in(normed, weight):
    gathered = lax.all_gather(normed, "col", axis=0, tiled=True)
    rows = gathered.shape[0] // lax.axis_size("grid")

    def term(start, count):
        return jnp.dot(gathered, weight, preferred_element_type=jnp.float32)

    return (
        gathered,
        lax.psum_scatter(
            term(jnp.int32(0), lax.axis_size("grid") * rows),
            "grid",
            scatter_dimension=0,
            tiled=True,
        ),
    )


def project_out(mixed, weight):
    gathered = lax.all_gather(mixed, "grid", axis=0, tiled=True)
    rows = gathered.shape[0] // lax.axis_size("col")

    def term(start, count):
        return jnp.dot(gathered, weight, preferred_element_type=jnp.float32)

    return (
        gathered,
        lax.psum_scatter(
            term(jnp.int32(0), lax.axis_size("col") * rows), "col", scatter_dimension=0, tiled=True
        ),
    )


def back_out(grad, weight, gathered_in):
    grad_all = lax.all_gather(grad, "col", axis=0, tiled=True)
    weight_grad = lax.dot_general(
        gathered_in, grad_all, (((0,), (0,)), ((), ())), preferred_element_type=jnp.float32
    )
    rows = grad_all.shape[0] // lax.axis_size("grid")

    def term(start, count):
        return lax.dot_general(
            grad_all, weight, (((1,), (1,)), ((), ())), preferred_element_type=jnp.float32
        )

    return (
        weight_grad,
        lax.psum_scatter(
            term(jnp.int32(0), lax.axis_size("grid") * rows),
            "grid",
            scatter_dimension=0,
            tiled=True,
        ),
    )


def back_in(grad, weight, gathered_in):
    grad_all = lax.all_gather(grad, "grid", axis=0, tiled=True)
    weight_grad = lax.dot_general(
        gathered_in, grad_all, (((0,), (0,)), ((), ())), preferred_element_type=jnp.float32
    )
    rows = grad_all.shape[0] // lax.axis_size("col")

    def term(start, count):
        return lax.dot_general(
            grad_all, weight, (((1,), (1,)), ((), ())), preferred_element_type=jnp.float32
        )

    return (
        weight_grad,
        lax.psum_scatter(
            term(jnp.int32(0), lax.axis_size("col") * rows), "col", scatter_dimension=0, tiled=True
        ),
    )


def gate_norm(mixed, gate, gain, bias):
    centre = jnp.mean(mixed, axis=-1, keepdims=True)
    centered = mixed - centre
    variance = jnp.mean(centered * centered, axis=-1, keepdims=True)
    normed = (centered * lax.rsqrt(variance + epsilon)).reshape(gate.shape) * gain + bias
    return jax.nn.silu(gate) * normed


def exact_gelu(values):
    return jax.nn.gelu(values, approximate=False)


def sum_rows(grads):
    return jax.tree.map(lambda part: part.astype(jnp.float32), lax.psum(shortened(grads), "row"))


def embed(part, index, count):
    blocks = (jnp.arange(count)[:, None] == index).astype(jnp.float32) * part[None, :]
    return blocks.reshape(-1)


def local_general(
    tokens,
    cotangent,
    lengths,
    deal_pages,
    land_slots,
    pre_gain,
    pre_bias,
    query_weight,
    key_weight,
    value_weight,
    gate_weight,
    group_gain,
    group_bias,
    output_weight,
    mid_gain,
    mid_bias,
    up_weight,
    down_weight,
):
    row_index = lax.axis_index("row")
    col_index = lax.axis_index("col")
    grid_index = lax.axis_index("grid")
    row_count = lax.axis_size("row")
    col_count = lax.axis_size("col")
    grid_count = lax.axis_size("grid")
    batches, tok_dev, half_width = tokens.shape
    page = tok_dev // row_count
    ranks = jnp.arange(row_count, dtype=jnp.int32)
    send_order = deal_pages[:, col_index, row_index, :]
    land_order = land_slots[:, col_index, row_index, :]
    land_inverse = jnp.sum(
        ranks[None, None, :] * (land_order[:, None, :] == ranks[None, :, None]).astype(jnp.int32),
        axis=2,
    )
    send_inverse = jnp.sum(
        ranks[None, None, :] * (send_order[:, None, :] == ranks[None, :, None]).astype(jnp.int32),
        axis=2,
    )
    pick = jax.vmap(lambda pages, order: jnp.take(pages, order, axis=0))

    def paged(values):
        return values.reshape(batches, row_count, page, half_width)

    arrived = (
        lax.all_to_all(
            pick(paged(tokens), send_order), "row", split_axis=1, concat_axis=1, tiled=True
        ),
        lax.all_to_all(
            pick(paged(cotangent), send_order), "row", split_axis=1, concat_axis=1, tiled=True
        ),
    )
    local_tokens = pick(arrived[0], land_inverse).reshape(batches, tok_dev, half_width)
    local_grads = pick(arrived[1], land_inverse).reshape(batches, tok_dev, half_width)
    in_weight = jnp.concatenate([query_weight, key_weight, value_weight, gate_weight], axis=1)
    qk_cols = query_weight.shape[1]
    v_cols = value_weight.shape[1]
    heads_dev = qk_cols // QK_HEAD
    head_ids = col_index * heads_dev + jnp.arange(heads_dev, dtype=jnp.int32)
    log_decay = jnp.log1p(-jnp.exp2(-5.0 - head_ids.astype(jnp.float32)))
    cell_len = tok_dev * col_count // grid_count
    cosines, sines = rotary_tables(cell_len, QK_HEAD)
    place = jnp.arange(cell_len, dtype=jnp.int32)
    results = []
    input_grads = []
    totals = None
    smalls = None
    for batch in range(batches):
        inputs = local_tokens[batch].astype(jnp.float32)
        norm_one, unit_one, spread_one = layer_stats_norm(inputs, pre_gain, pre_bias)
        gathered_one, projected = project_in(norm_one.astype(jnp.bfloat16), in_weight)
        query_raw = projected[:, :qk_cols].reshape(cell_len, heads_dev, QK_HEAD)
        key_raw = projected[:, qk_cols : 2 * qk_cols].reshape(cell_len, heads_dev, QK_HEAD)
        value_raw = projected[:, 2 * qk_cols : 2 * qk_cols + v_cols]
        gate_raw = projected[:, 2 * qk_cols + v_cols :]
        query_low = (query_raw * cosines + turn(query_raw) * sines).astype(jnp.bfloat16)
        key_low = (key_raw * cosines + turn(key_raw) * sines).astype(jnp.bfloat16)
        value_low = value_raw.astype(jnp.bfloat16).reshape(cell_len, heads_dev, V_HEAD)
        ends = jnp.cumsum(lengths[batch, row_index, grid_index])
        segment = jnp.sum((place[:, None] >= ends[None, :]).astype(jnp.int32), axis=1)
        mixed, states = retention_forward(query_low, key_low, value_low, segment, log_decay, CH)
        unit_out, gate_pull = jax.vjp(gate_norm, mixed, gate_raw, group_gain, group_bias)
        gathered_two, attn_out = project_out(unit_out.astype(jnp.bfloat16), output_weight)
        resid = inputs + attn_out
        norm_two, unit_two, spread_two = layer_stats_norm(resid, mid_gain, mid_bias)
        gathered_three, pre_act = project_in(norm_two.astype(jnp.bfloat16), up_weight)
        activated, gelu_pull = jax.vjp(exact_gelu, pre_act)
        gathered_four, ffn_out = project_out(activated.astype(jnp.bfloat16), down_weight)
        results.append((resid + ffn_out).astype(jnp.bfloat16))
        top_grad = local_grads[batch]
        down_part, grad_act = back_out(top_grad, down_weight, gathered_four)
        (grad_pre,) = gelu_pull(grad_act)
        up_part, grad_norm_two = back_in(grad_pre.astype(jnp.bfloat16), up_weight, gathered_three)
        resid_part, mid_gain_part, mid_bias_part = norm_back(
            grad_norm_two, unit_two, spread_two, mid_gain
        )
        grad_resid = top_grad.astype(jnp.float32) + resid_part
        out_part, grad_unit = back_out(grad_resid.astype(jnp.bfloat16), output_weight, gathered_two)
        grad_mixed, grad_gate, group_gain_part, group_bias_part = gate_pull(grad_unit)
        grad_query, grad_key, grad_value = retention_backward(
            query_low,
            key_low,
            value_low,
            segment,
            states,
            grad_mixed.astype(jnp.bfloat16),
            log_decay,
            CH,
        )
        grad_query = grad_query * cosines + turn_back(grad_query * sines)
        grad_key = grad_key * cosines + turn_back(grad_key * sines)
        grad_proj = jnp.concatenate(
            [
                grad_query.reshape(cell_len, qk_cols),
                grad_key.reshape(cell_len, qk_cols),
                grad_value.reshape(cell_len, v_cols),
                grad_gate,
            ],
            axis=1,
        ).astype(jnp.bfloat16)
        in_part, grad_norm_one = back_in(grad_proj, in_weight, gathered_one)
        input_part, pre_gain_part, pre_bias_part = norm_back(
            grad_norm_one, unit_one, spread_one, pre_gain
        )
        input_grads.append((grad_resid + input_part).astype(jnp.bfloat16))
        parts = (in_part, out_part, up_part, down_part)
        totals = (
            parts if totals is None else tuple((total + part for total, part in zip(totals, parts)))
        )
        small_parts = (
            pre_gain_part,
            pre_bias_part,
            mid_gain_part,
            mid_bias_part,
            group_gain_part,
            group_bias_part,
        )
        smalls = (
            small_parts
            if smalls is None
            else tuple((total + part for total, part in zip(smalls, small_parts)))
        )
    totals = sum_rows(totals)
    in_total, out_total, up_total, down_total = totals
    feature_len = pre_gain.shape[0]
    group_len = group_gain.shape[0]
    spread_out = (
        embed(smalls[0], grid_index, grid_count),
        embed(smalls[1], grid_index, grid_count),
        embed(smalls[2], grid_index, grid_count),
        embed(smalls[3], grid_index, grid_count),
        embed(smalls[4], col_index, col_count),
        embed(smalls[5], col_index, col_count),
    )
    summed = lax.psum(
        (spread_out[0], spread_out[1], spread_out[2], spread_out[3], spread_out[4], spread_out[5]),
        ("row", "col", "grid"),
    )
    pregain_grad = lax.dynamic_slice_in_dim(summed[0], grid_index * feature_len, feature_len)
    prebias_grad = lax.dynamic_slice_in_dim(summed[1], grid_index * feature_len, feature_len)
    midgain_grad = lax.dynamic_slice_in_dim(summed[2], grid_index * feature_len, feature_len)
    midbias_grad = lax.dynamic_slice_in_dim(summed[3], grid_index * feature_len, feature_len)
    groupgain_grad = lax.dynamic_slice_in_dim(summed[4], col_index * group_len, group_len)
    groupbias_grad = lax.dynamic_slice_in_dim(summed[5], col_index * group_len, group_len)
    result_all = jnp.stack(results)
    grad_all = jnp.stack(input_grads)
    returned = (
        lax.all_to_all(
            pick(paged(result_all), land_order), "row", split_axis=1, concat_axis=1, tiled=True
        ),
        lax.all_to_all(
            pick(paged(grad_all), land_order), "row", split_axis=1, concat_axis=1, tiled=True
        ),
    )
    block_out = pick(returned[0], send_inverse).reshape(batches, tok_dev, half_width)
    tokens_grad = pick(returned[1], send_inverse).reshape(batches, tok_dev, half_width)
    query_grad = in_total[:, :qk_cols]
    key_grad = in_total[:, qk_cols : 2 * qk_cols]
    value_grad = in_total[:, 2 * qk_cols : 2 * qk_cols + v_cols]
    gating_grad = in_total[:, 2 * qk_cols + v_cols :]
    return (
        block_out,
        tokens_grad,
        pregain_grad,
        prebias_grad,
        query_grad,
        key_grad,
        value_grad,
        gating_grad,
        groupgain_grad,
        groupbias_grad,
        out_total,
        midgain_grad,
        midbias_grad,
        up_total,
        down_total,
    )


def swap(values, axis, bit):
    count = lax.axis_size(axis)
    return lax.ppermute(values, axis, [(one, one ^ bit) for one in range(count)])


def gather_cell(own):
    far = swap(own, "col", 2)
    near = swap(own, "col", 1)
    across = swap(far, "col", 1)
    return jnp.concatenate([own, near, far, across], axis=0)


def scatter_cell(part):
    rows = part.shape[0] // 4
    outer = swap(part[3 * rows :], "col", 1)
    away = part[2 * rows : 3 * rows].astype(jnp.float32) + outer.astype(jnp.float32)
    far = swap(away.astype(jnp.bfloat16), "col", 2)
    near = swap(part[rows : 2 * rows], "col", 1)
    return part[:rows].astype(jnp.float32) + near.astype(jnp.float32) + far.astype(jnp.float32)


def dot(left, right, left_axis=1, right_axis=0):
    return lax.dot_general(
        left, right, (((left_axis,), (right_axis,)), ((), ())), preferred_element_type=jnp.float32
    )


def page_routes(back):
    rows, cols, grids = lax.axis_size("row"), lax.axis_size("col"), lax.axis_size("grid")
    routes = []
    for step in range(4):
        pairs = []
        for row in range(rows):
            for col in range(cols):
                for grid in range(grids):
                    source = (row * cols + col) * grids + grid
                    to_row = (2 * (row // 2) + grid) ^ step
                    to_col = 2 * (col % 2) + row % 2
                    target = (to_row * cols + to_col) * grids + col // 2
                    pairs.append((target, source) if back else (source, target))
        routes.append(pairs)
    return routes


def cell_norm(values, gain, bias):
    centre = jnp.mean(values, axis=1, keepdims=True)
    spread = lax.rsqrt(jnp.mean(values * values, axis=1, keepdims=True) - centre * centre + epsilon)
    normal = (values - centre) * spread
    return ((normal * gain + bias).astype(jnp.bfloat16), normal, spread)


def cell_norm_back(grad, normal, spread, gain):
    scaled = grad * gain
    first = jnp.mean(scaled, axis=1, keepdims=True)
    second = jnp.mean(scaled * normal, axis=1, keepdims=True)
    back = (scaled - first - normal * second) * spread
    return (back, jnp.sum(grad * normal, axis=0), jnp.sum(grad, axis=0))


def rotate(values, cosines, sines):
    half = values.shape[1] // 2
    low, high = values[:, :half], values[:, half:]
    return jnp.concatenate([low * cosines - high * sines, high * cosines + low * sines], axis=1)


def rotate_back(values, cosines, sines):
    half = values.shape[1] // 2
    low, high = values[:, :half], values[:, half:]
    return jnp.concatenate([low * cosines + high * sines, high * cosines - low * sines], axis=1)


def head_cell(query, keys, values, decay, cross, state, scale):
    weights = (dot(query, keys, 1, 1) * scale * decay).astype(jnp.bfloat16)
    scaled = (query.astype(jnp.float32) * (cross * scale)).astype(jnp.bfloat16)
    mixed = dot(weights, values) + dot(scaled, state.astype(jnp.bfloat16))
    return (mixed, weights)


def head_cell_back(query, keys, values, weights, decay, cross, keep, state, grad_state, grad, scale):
    grad_raw = (dot(grad, values, 1, 1) * decay * scale).astype(jnp.bfloat16)
    grad_added = grad_state.astype(jnp.bfloat16)
    kept = (keys.astype(jnp.float32) * keep).astype(jnp.bfloat16)
    grad_query = dot(grad_raw, keys) + dot(grad, state.astype(jnp.bfloat16), 1, 1) * (cross * scale)
    grad_keys = dot(grad_raw, query, 0, 0) + dot(values, grad_added, 1, 1) * keep
    grad_values = dot(weights, grad, 0, 0) + dot(kept, grad_added)
    return (grad_query, grad_keys, grad_values)


def local_cells(
    tokens,
    cotangent,
    lengths,
    deal_pages,
    land_slots,
    pre_gain,
    pre_bias,
    query_weight,
    key_weight,
    value_weight,
    gate_weight,
    group_gain,
    group_bias,
    output_weight,
    mid_gain,
    mid_bias,
    up_weight,
    down_weight,
):
    row_index = lax.axis_index("row")
    col_index = lax.axis_index("col")
    grid_index = lax.axis_index("grid")
    col_count = lax.axis_size("col")
    grid_count = lax.axis_size("grid")
    batches, tok_dev, half_width = tokens.shape
    page = tok_dev // 4
    cell_len = 2 * tok_dev
    qk_cols = query_weight.shape[1]
    v_cols = value_weight.shape[1]
    heads_dev = qk_cols // QK_HEAD
    scale = QK_HEAD ** (-0.5)
    everywhere = ("row", "col", "grid")
    pick = jax.vmap(lambda pages, order: jnp.take(pages, order, axis=0))

    steps = jnp.arange(4, dtype=jnp.int32)
    to_rows = (2 * (row_index // 2) + grid_index) ^ steps
    sent_pages = deal_pages[:, col_index, row_index, :][:, to_rows]
    routes, returns = page_routes(False), page_routes(True)
    half_swap = (row_index + grid_index) % 2

    def spread_pages(values):
        chosen = pick(values.reshape(batches, 4, page, half_width), sent_pages)
        got = [lax.ppermute(chosen[:, step], everywhere, routes[step]) for step in range(4)]
        pairs = []
        for place in range(2):
            one, two = got[2 * place], got[2 * place + 1]
            pairs.append(
                jnp.concatenate(
                    [jnp.where(half_swap == 0, one, two), jnp.where(half_swap == 0, two, one)], axis=2
                )
            )
        return jnp.concatenate(pairs, axis=1)

    from_row = jnp.argmax(
        deal_pages[:, col_index, row_index, None, :] == steps[None, :, None], axis=2
    ).astype(jnp.int32)
    from_step = from_row ^ (2 * (row_index // 2) + grid_index)

    def return_pages(values):
        got = []
        for step in range(4):
            rows = values[:, (step // 2) * page : (step // 2 + 1) * page]
            first, second = rows[..., :half_width], rows[..., half_width:]
            sent = jnp.where((half_swap + step) % 2 == 0, first, second)
            got.append(lax.ppermute(sent, everywhere, returns[step]))
        return pick(jnp.stack(got, axis=1), from_step).reshape(batches, tok_dev, half_width)

    local_tokens = spread_pages(tokens)
    local_grads = spread_pages(cotangent)

    def both(values, axis):
        return jnp.concatenate([values, swap(values, "grid", 1)], axis=axis)

    pre_gain_all, pre_bias_all = both(pre_gain, 0), both(pre_bias, 0)
    mid_gain_all, mid_bias_all = both(mid_gain, 0), both(mid_bias, 0)
    query_all, key_all = both(query_weight, 0), both(key_weight, 0)
    value_all, gate_all = both(value_weight, 0), both(gate_weight, 0)
    output_all = both(output_weight, 1)
    up_all = both(up_weight, 0)
    down_all = both(down_weight, 1)

    head_ids = col_index * heads_dev + jnp.arange(heads_dev, dtype=jnp.int32)
    log_decay = jnp.log1p(-jnp.exp2(-5.0 - head_ids.astype(jnp.float32)))
    rates = 10000.0 ** (-jnp.arange(QK_HEAD // 2).astype(jnp.float32) / (QK_HEAD // 2))
    x_index, core_index = col_index // 2, col_index % 2
    inner = jnp.arange(page, dtype=jnp.int32)
    places = []
    tables = []
    for batch in range(batches):
        chunks = []
        for ahead in range(2):
            for beside in range(2):
                group = x_index ^ ahead
                for place in range(2):
                    source = 2 * ((row_index // 2) ^ place) + (core_index ^ beside)
                    slot = land_slots[batch, 2 * grid_index + group, row_index, source]
                    chunks.append(tok_dev * group + page * slot + inner)
        position = jnp.concatenate(chunks)
        angles = position.astype(jnp.float32)[:, None] * rates[None, :]
        ends = jnp.cumsum(lengths[batch, row_index, grid_index])
        segment = jnp.sum((position[:, None] >= ends[None, :]).astype(jnp.int32), axis=1)
        last = jnp.sum((cell_len - 1 >= ends).astype(jnp.int32))
        distance = position[:, None] - position[None, :]
        same = (segment[:, None] == segment[None, :]) & (distance >= 0)
        span = jnp.maximum(distance, 0).astype(jnp.float32)
        decays = [
            jnp.where(same, jnp.exp(log_decay[head] * span), 0.0) for head in range(heads_dev)
        ]
        crosses = [
            jnp.where(
                segment == -1, jnp.exp(log_decay[head] * (position + 1).astype(jnp.float32)), 0.0
            )[:, None]
            for head in range(heads_dev)
        ]
        keeps = [
            jnp.where(
                segment == last,
                jnp.exp(log_decay[head] * (cell_len - 1 - position).astype(jnp.float32)),
                0.0,
            )[:, None]
            for head in range(heads_dev)
        ]
        tables.append((jnp.cos(angles), jnp.sin(angles), decays, crosses, keeps))
    state = jnp.zeros((QK_HEAD, V_HEAD), jnp.float32)
    grad_state = jnp.zeros((QK_HEAD, V_HEAD), jnp.float32)

    saved = []
    results = []
    for batch in range(batches):
        cosines, sines, decays, crosses, keeps = tables[batch]
        inputs = local_tokens[batch].astype(jnp.float32)
        hidden_one, unit_one, spread_one = cell_norm(inputs, pre_gain_all, pre_bias_all)
        cell_one = gather_cell(hidden_one)
        query_raw, key_raw = dot(cell_one, query_all), dot(cell_one, key_all)
        value_low = dot(cell_one, value_all).astype(jnp.bfloat16)
        gate = dot(cell_one, gate_all)
        heads = []
        gated = []
        for head in range(heads_dev):
            qk = slice(head * QK_HEAD, (head + 1) * QK_HEAD)
            vs = slice(head * V_HEAD, (head + 1) * V_HEAD)
            query = rotate(query_raw[:, qk], cosines, sines).astype(jnp.bfloat16)
            keys = rotate(key_raw[:, qk], cosines, sines).astype(jnp.bfloat16)
            values = value_low[:, vs]
            mixed, weights = head_cell(
                query, keys, values, decays[head], crosses[head], state, scale
            )
            centred = mixed - jnp.mean(mixed, axis=1, keepdims=True)
            spread = lax.rsqrt(jnp.mean(centred * centred, axis=1, keepdims=True) + epsilon)
            normal = centred * spread
            scaled = normal * group_gain[vs] + group_bias[vs]
            gate_part = gate[:, vs]
            gated.append((gate_part * jax.nn.sigmoid(gate_part) * scaled).astype(jnp.bfloat16))
            heads.append((query, keys, values, weights, normal, spread, gate_part))
        unit_out = jnp.concatenate(gated, axis=1)
        attn_out = scatter_cell(dot(unit_out, output_all).astype(jnp.bfloat16))
        resid = inputs + attn_out
        hidden_two, unit_two, spread_two = cell_norm(resid, mid_gain_all, mid_bias_all)
        cell_two = gather_cell(hidden_two)
        pre_act = dot(cell_two, up_all)
        activated, gelu_pull = jax.vjp(exact_gelu, pre_act)
        activated = activated.astype(jnp.bfloat16)
        ffn_out = scatter_cell(dot(activated, down_all).astype(jnp.bfloat16))
        results.append((resid + ffn_out).astype(jnp.bfloat16))
        saved.append(
            (
                unit_one,
                spread_one,
                cell_one,
                heads,
                unit_out,
                unit_two,
                spread_two,
                cell_two,
                activated,
                gelu_pull,
            )
        )
    block_out = return_pages(jnp.stack(results))

    input_grads = []
    smalls = []
    top_cells = []
    pre_grads = []
    mid_cells = []
    proj_grads = []
    for batch in range(batches):
        cosines, sines, decays, crosses, keeps = tables[batch]
        (
            unit_one,
            spread_one,
            cell_one,
            heads,
            unit_out,
            unit_two,
            spread_two,
            cell_two,
            activated,
            gelu_pull,
        ) = saved[batch]
        top_grad = local_grads[batch]
        top_cell = gather_cell(top_grad)
        (grad_pre,) = gelu_pull(dot(top_cell, down_all, 1, 1))
        grad_pre = grad_pre.astype(jnp.bfloat16)
        grad_two = scatter_cell(dot(grad_pre, up_all, 1, 1).astype(jnp.bfloat16))
        back_two, mid_gain_part, mid_bias_part = cell_norm_back(
            grad_two, unit_two, spread_two, mid_gain_all
        )
        grad_resid = top_grad.astype(jnp.float32) + back_two
        mid_cell = gather_cell(grad_resid.astype(jnp.bfloat16))
        grad_unit = dot(mid_cell, output_all, 1, 1)
        query_parts, key_parts, value_parts, gate_parts = [], [], [], []
        group_gain_parts, group_bias_parts = [], []
        for head in range(heads_dev):
            vs = slice(head * V_HEAD, (head + 1) * V_HEAD)
            query, keys, values, weights, normal, spread, gate_part = heads[head]
            grad_u = grad_unit[:, vs]
            sig = jax.nn.sigmoid(gate_part)
            scaled = normal * group_gain[vs] + group_bias[vs]
            gate_parts.append(
                (grad_u * scaled * (sig * (1.0 + gate_part * (1.0 - sig)))).astype(jnp.bfloat16)
            )
            grad_scaled = grad_u * (gate_part * sig)
            group_gain_parts.append(jnp.sum(grad_scaled * normal, axis=0))
            group_bias_parts.append(jnp.sum(grad_scaled, axis=0))
            grad_normal = grad_scaled * group_gain[vs]
            grad_mixed = spread * (
                grad_normal
                - jnp.mean(grad_normal, axis=1, keepdims=True)
                - normal * jnp.mean(grad_normal * normal, axis=1, keepdims=True)
            )
            grad_query, grad_keys, grad_values = head_cell_back(
                query,
                keys,
                values,
                weights,
                decays[head],
                crosses[head],
                keeps[head],
                state,
                grad_state,
                grad_mixed.astype(jnp.bfloat16),
                scale,
            )
            query_parts.append(rotate_back(grad_query, cosines, sines).astype(jnp.bfloat16))
            key_parts.append(rotate_back(grad_keys, cosines, sines).astype(jnp.bfloat16))
            value_parts.append(grad_values.astype(jnp.bfloat16))
        grad_q = jnp.concatenate(query_parts, axis=1)
        grad_k = jnp.concatenate(key_parts, axis=1)
        grad_v = jnp.concatenate(value_parts, axis=1)
        grad_g = jnp.concatenate(gate_parts, axis=1)
        grad_cell = (
            dot(grad_q, query_all, 1, 1)
            + dot(grad_k, key_all, 1, 1)
            + dot(grad_v, value_all, 1, 1)
            + dot(grad_g, gate_all, 1, 1)
        )
        grad_one = scatter_cell(grad_cell.astype(jnp.bfloat16))
        back_one, pre_gain_part, pre_bias_part = cell_norm_back(
            grad_one, unit_one, spread_one, pre_gain_all
        )
        input_grads.append((grad_resid + back_one).astype(jnp.bfloat16))
        top_cells.append(top_cell)
        pre_grads.append(grad_pre)
        mid_cells.append(mid_cell)
        proj_grads.append((grad_q, grad_k, grad_v, grad_g))
        smalls.append(
            (
                pre_gain_part,
                pre_bias_part,
                mid_gain_part,
                mid_bias_part,
                jnp.concatenate(group_gain_parts),
                jnp.concatenate(group_bias_parts),
            )
        )
    tokens_grad = return_pages(jnp.stack(input_grads))

    def over_rows(grad, axis):
        half = grad.shape[axis] // 2
        own = lax.slice_in_dim(grad, 0, half, axis=axis)
        other = lax.slice_in_dim(grad, half, 2 * half, axis=axis).astype(jnp.bfloat16)
        pair = own + swap(other, "grid", 1).astype(jnp.float32)
        return lax.psum(pair.astype(jnp.bfloat16), "row").astype(jnp.float32)

    def tall(parts):
        return jnp.concatenate(parts, axis=0)

    down_grad = over_rows(dot(tall([one[8] for one in saved]), tall(top_cells), 0, 0), 1)
    up_grad = over_rows(dot(tall([one[7] for one in saved]), tall(pre_grads), 0, 0), 0)
    out_grad = over_rows(dot(tall([one[4] for one in saved]), tall(mid_cells), 0, 0), 1)
    cells = tall([one[2] for one in saved])
    query_grad, key_grad, value_grad, gating_grad = [
        over_rows(dot(cells, tall([one[part] for one in proj_grads]), 0, 0), 0) for part in range(4)
    ]

    totals = [sum(parts) for parts in zip(*smalls)]
    feature_len = pre_gain.shape[0]
    group_len = group_gain.shape[0]

    def in_place(part):
        return jnp.where(grid_index == 0, part, jnp.roll(part, feature_len))

    summed = lax.psum(
        tuple(in_place(part) for part in totals[:4])
        + tuple(embed(part, col_index, col_count) for part in totals[4:]),
        everywhere,
    )
    features = [
        lax.dynamic_slice_in_dim(part, grid_index * feature_len, feature_len) for part in summed[:4]
    ]
    groups = [
        lax.dynamic_slice_in_dim(part, col_index * group_len, group_len) for part in summed[4:]
    ]
    return (
        block_out,
        tokens_grad,
        features[0],
        features[1],
        query_grad,
        key_grad,
        value_grad,
        gating_grad,
        groups[0],
        groups[1],
        out_grad,
        features[2],
        features[3],
        up_grad,
        down_grad,
    )


def local(*arguments):
    tokens, query_weight = arguments[0], arguments[7]
    sizes = tuple(lax.axis_size(axis) for axis in ("row", "col", "grid"))
    one_block = 2 * tokens.shape[1] == CH
    if sizes == (4, 4, 2) and one_block and query_weight.shape[1] % QK_HEAD == 0:
        return local_cells(*arguments)
    return local_general(*arguments)


def solution(mesh):
    placed = (
        P(None, ("row", "col"), "grid"),
        P(None, ("row", "col"), "grid"),
        P(),
        P(),
        P(),
        P("grid"),
        P("grid"),
        P("grid", "col"),
        P("grid", "col"),
        P("grid", "col"),
        P("grid", "col"),
        P("col"),
        P("col"),
        P("col", "grid"),
        P("grid"),
        P("grid"),
        P("grid", "col"),
        P("col", "grid"),
    )
    return jax.shard_map(
        local,
        mesh=mesh,
        in_specs=placed,
        out_specs=(
            P(None, ("row", "col"), "grid"),
            P(None, ("row", "col"), "grid"),
            P("grid"),
            P("grid"),
            P("grid", "col"),
            P("grid", "col"),
            P("grid", "col"),
            P("grid", "col"),
            P("col"),
            P("col"),
            P("col", "grid"),
            P("grid"),
            P("grid"),
            P("grid", "col"),
            P("col", "grid"),
        ),
        check_vma=False,
    )
```

```python
import jax
import jax.numpy as jnp
from jax import lax
from jax.experimental import pallas as pl
from jax.experimental.pallas import tpu as pltpu
from jax.sharding import PartitionSpec as P

D = 2048
QK_HEAD = 256
V_HEAD = 512
CH = 512


epsilon = 1e-05


def shortened(array):

    def short(part):
        return part.astype(jnp.bfloat16) if part.dtype == jnp.float32 else part

    return jax.tree.map(short, array)


def turn(values):
    half = values.shape[-1] // 2
    return jnp.concatenate([-values[..., half:], values[..., :half]], axis=-1)


def turn_back(values):
    half = values.shape[-1] // 2
    return jnp.concatenate([values[..., half:], -values[..., :half]], axis=-1)


def rotary_tables(length, width):
    positions = jnp.arange(length, dtype=jnp.int32).astype(jnp.float32)
    rates = 10000.0 ** (-jnp.arange(width // 2).astype(jnp.float32) / (width // 2))
    angles = positions[:, None] * rates[None, :]
    angles = jnp.concatenate([angles, angles], axis=1)[:, None, :]
    return (jnp.cos(angles), jnp.sin(angles))


def block_masks(segment, previous, log_decay, block):
    place = jnp.arange(block, dtype=jnp.int32)
    distance = place[:, None] - place[None, :]
    same = (segment[:, None] == segment[None, :]) & (distance >= 0)
    decay = jnp.where(
        same[None],
        jnp.exp(log_decay[:, None, None] * jnp.maximum(distance, 0)[None].astype(jnp.float32)),
        0.0,
    )
    cross = jnp.where(
        (segment == previous)[None, :],
        jnp.exp(log_decay[:, None] * (place + 1)[None].astype(jnp.float32)),
        0.0,
    )
    last = segment[block - 1]
    keep = jnp.where(
        (segment == last)[None, :],
        jnp.exp(log_decay[:, None] * (block - 1 - place)[None].astype(jnp.float32)),
        0.0,
    )
    carry_weight = jnp.where(last == previous, jnp.exp(log_decay * block), 0.0)
    return (decay, cross, keep, carry_weight, last)


def retention_forward(query, keys, values, segment, log_decay, block):
    length, heads, width = query.shape
    blocks = length // block
    scale = width ** (-0.5)
    split = (
        query.reshape(blocks, block, heads, width),
        keys.reshape(blocks, block, heads, width),
        values.reshape(blocks, block, heads, values.shape[2]),
        segment.reshape(blocks, block),
    )

    def advance(carry, pieces):
        state, previous = carry
        query_b, keys_b, values_b, segment_b = pieces
        decay, cross, keep, carry_weight, last = block_masks(segment_b, previous, log_decay, block)
        raw = jnp.einsum("ihd,jhd->hij", query_b, keys_b, preferred_element_type=jnp.float32)
        weights = (raw * scale * decay).astype(jnp.bfloat16)
        inner = jnp.einsum("hij,jhe->ihe", weights, values_b, preferred_element_type=jnp.float32)
        scaled = (query_b.astype(jnp.float32) * (cross.T[:, :, None] * scale)).astype(jnp.bfloat16)
        outer = jnp.einsum(
            "ihd,hde->ihe", scaled, state.astype(jnp.bfloat16), preferred_element_type=jnp.float32
        )
        kept = (keys_b.astype(jnp.float32) * keep.T[:, :, None]).astype(jnp.bfloat16)
        added = jnp.einsum("jhd,jhe->hde", kept, values_b, preferred_element_type=jnp.float32)
        new_state = carry_weight[:, None, None] * state + added
        return ((new_state, last), (inner + outer, state))

    start = (jnp.zeros((heads, width, values.shape[2]), jnp.float32), jnp.array(-1, jnp.int32))
    _, (outputs, states) = lax.scan(advance, start, split)
    return (outputs.reshape(length, heads, values.shape[2]), states)


def retention_backward(query, keys, values, segment, states, grad_out, log_decay, block):
    length, heads, width = query.shape
    vwidth = values.shape[2]
    blocks = length // block
    scale = width ** (-0.5)
    segment_blocks = segment.reshape(blocks, block)
    previous_all = jnp.concatenate([jnp.full((1,), -1, jnp.int32), segment_blocks[:-1, -1]])
    split = (
        query.reshape(blocks, block, heads, width),
        keys.reshape(blocks, block, heads, width),
        values.reshape(blocks, block, heads, vwidth),
        segment_blocks,
        previous_all,
        states,
        grad_out.reshape(blocks, block, heads, vwidth),
    )

    def retreat(grad_state, pieces):
        query_b, keys_b, values_b, segment_b, previous, state, grad_b = pieces
        decay, cross, keep, carry_weight, last = block_masks(segment_b, previous, log_decay, block)
        raw = jnp.einsum("ihd,jhd->hij", query_b, keys_b, preferred_element_type=jnp.float32)
        weights = (raw * scale * decay).astype(jnp.bfloat16)
        grad_weights = jnp.einsum(
            "ihe,jhe->hij", grad_b, values_b, preferred_element_type=jnp.float32
        )
        grad_raw = (grad_weights * decay * scale).astype(jnp.bfloat16)
        grad_query = jnp.einsum(
            "hij,jhd->ihd", grad_raw, keys_b, preferred_element_type=jnp.float32
        )
        grad_keys = jnp.einsum(
            "hij,ihd->jhd", grad_raw, query_b, preferred_element_type=jnp.float32
        )
        grad_values = jnp.einsum(
            "hij,ihe->jhe", weights, grad_b, preferred_element_type=jnp.float32
        )
        scaled = (query_b.astype(jnp.float32) * (cross.T[:, :, None] * scale)).astype(jnp.bfloat16)
        grad_scaled = jnp.einsum(
            "ihe,hde->ihd", grad_b, state.astype(jnp.bfloat16), preferred_element_type=jnp.float32
        )
        grad_query = grad_query + grad_scaled * (cross.T[:, :, None] * scale)
        grad_state_low = jnp.einsum(
            "ihd,ihe->hde", scaled, grad_b, preferred_element_type=jnp.float32
        )
        grad_added = grad_state.astype(jnp.bfloat16)
        kept = (keys_b.astype(jnp.float32) * keep.T[:, :, None]).astype(jnp.bfloat16)
        grad_kept = jnp.einsum(
            "jhe,hde->jhd", values_b, grad_added, preferred_element_type=jnp.float32
        )
        grad_keys = grad_keys + grad_kept * keep.T[:, :, None]
        grad_values = grad_values + jnp.einsum(
            "jhd,hde->jhe", kept, grad_added, preferred_element_type=jnp.float32
        )
        new_grad = carry_weight[:, None, None] * grad_state + grad_state_low
        return (new_grad, (grad_query, grad_keys, grad_values))

    start = jnp.zeros((heads, width, vwidth), jnp.float32)
    _, (grad_query, grad_keys, grad_values) = lax.scan(retreat, start, split, reverse=True)
    return (
        grad_query.reshape(length, heads, width),
        grad_keys.reshape(length, heads, width),
        grad_values.reshape(length, heads, vwidth),
    )


def feature_sums(first, second):
    return lax.psum((first, second), "grid")


def layer_stats_norm(values, gain, bias):
    first, second = feature_sums(jnp.sum(values, axis=1), jnp.sum(values * values, axis=1))
    centre = first / D
    spread = lax.rsqrt(second / D - centre * centre + epsilon)
    normal = (values - centre[:, None]) * spread[:, None]
    return (normal * gain + bias, normal, spread)


def norm_back(grad, normal, spread, gain):
    scaled = grad * gain
    first, second = feature_sums(jnp.sum(scaled, axis=1), jnp.sum(scaled * normal, axis=1))
    back = (scaled - first[:, None] / D - normal * (second[:, None] / D)) * spread[:, None]
    return (back, jnp.sum(grad * normal, axis=0), jnp.sum(grad, axis=0))


def project_in(normed, weight):
    gathered = lax.all_gather(normed, "col", axis=0, tiled=True)
    rows = gathered.shape[0] // lax.axis_size("grid")

    def term(start, count):
        return jnp.dot(gathered, weight, preferred_element_type=jnp.float32)

    return (
        gathered,
        lax.psum_scatter(
            term(jnp.int32(0), lax.axis_size("grid") * rows),
            "grid",
            scatter_dimension=0,
            tiled=True,
        ),
    )


def project_out(mixed, weight):
    gathered = lax.all_gather(mixed, "grid", axis=0, tiled=True)
    rows = gathered.shape[0] // lax.axis_size("col")

    def term(start, count):
        return jnp.dot(gathered, weight, preferred_element_type=jnp.float32)

    return (
        gathered,
        lax.psum_scatter(
            term(jnp.int32(0), lax.axis_size("col") * rows), "col", scatter_dimension=0, tiled=True
        ),
    )


def back_out(grad, weight, gathered_in):
    grad_all = lax.all_gather(grad, "col", axis=0, tiled=True)
    weight_grad = lax.dot_general(
        gathered_in, grad_all, (((0,), (0,)), ((), ())), preferred_element_type=jnp.float32
    )
    rows = grad_all.shape[0] // lax.axis_size("grid")

    def term(start, count):
        return lax.dot_general(
            grad_all, weight, (((1,), (1,)), ((), ())), preferred_element_type=jnp.float32
        )

    return (
        weight_grad,
        lax.psum_scatter(
            term(jnp.int32(0), lax.axis_size("grid") * rows),
            "grid",
            scatter_dimension=0,
            tiled=True,
        ),
    )


def back_in(grad, weight, gathered_in):
    grad_all = lax.all_gather(grad, "grid", axis=0, tiled=True)
    weight_grad = lax.dot_general(
        gathered_in, grad_all, (((0,), (0,)), ((), ())), preferred_element_type=jnp.float32
    )
    rows = grad_all.shape[0] // lax.axis_size("col")

    def term(start, count):
        return lax.dot_general(
            grad_all, weight, (((1,), (1,)), ((), ())), preferred_element_type=jnp.float32
        )

    return (
        weight_grad,
        lax.psum_scatter(
            term(jnp.int32(0), lax.axis_size("col") * rows), "col", scatter_dimension=0, tiled=True
        ),
    )


def gate_norm(mixed, gate, gain, bias):
    centre = jnp.mean(mixed, axis=-1, keepdims=True)
    centered = mixed - centre
    variance = jnp.mean(centered * centered, axis=-1, keepdims=True)
    normed = (centered * lax.rsqrt(variance + epsilon)).reshape(gate.shape) * gain + bias
    return jax.nn.silu(gate) * normed


def exact_gelu(values):
    return jax.nn.gelu(values, approximate=False)


def sum_rows(grads):
    return jax.tree.map(lambda part: part.astype(jnp.float32), lax.psum(shortened(grads), "row"))


def embed(part, index, count):
    blocks = (jnp.arange(count)[:, None] == index).astype(jnp.float32) * part[None, :]
    return blocks.reshape(-1)


def local_general(
    tokens,
    cotangent,
    lengths,
    deal_pages,
    land_slots,
    pre_gain,
    pre_bias,
    query_weight,
    key_weight,
    value_weight,
    gate_weight,
    group_gain,
    group_bias,
    output_weight,
    mid_gain,
    mid_bias,
    up_weight,
    down_weight,
):
    row_index = lax.axis_index("row")
    col_index = lax.axis_index("col")
    grid_index = lax.axis_index("grid")
    row_count = lax.axis_size("row")
    col_count = lax.axis_size("col")
    grid_count = lax.axis_size("grid")
    batches, tok_dev, half_width = tokens.shape
    page = tok_dev // row_count
    ranks = jnp.arange(row_count, dtype=jnp.int32)
    send_order = deal_pages[:, col_index, row_index, :]
    land_order = land_slots[:, col_index, row_index, :]
    land_inverse = jnp.sum(
        ranks[None, None, :] * (land_order[:, None, :] == ranks[None, :, None]).astype(jnp.int32),
        axis=2,
    )
    send_inverse = jnp.sum(
        ranks[None, None, :] * (send_order[:, None, :] == ranks[None, :, None]).astype(jnp.int32),
        axis=2,
    )
    pick = jax.vmap(lambda pages, order: jnp.take(pages, order, axis=0))

    def paged(values):
        return values.reshape(batches, row_count, page, half_width)

    arrived = (
        lax.all_to_all(
            pick(paged(tokens), send_order), "row", split_axis=1, concat_axis=1, tiled=True
        ),
        lax.all_to_all(
            pick(paged(cotangent), send_order), "row", split_axis=1, concat_axis=1, tiled=True
        ),
    )
    local_tokens = pick(arrived[0], land_inverse).reshape(batches, tok_dev, half_width)
    local_grads = pick(arrived[1], land_inverse).reshape(batches, tok_dev, half_width)
    in_weight = jnp.concatenate([query_weight, key_weight, value_weight, gate_weight], axis=1)
    qk_cols = query_weight.shape[1]
    v_cols = value_weight.shape[1]
    heads_dev = qk_cols // QK_HEAD
    head_ids = col_index * heads_dev + jnp.arange(heads_dev, dtype=jnp.int32)
    log_decay = jnp.log1p(-jnp.exp2(-5.0 - head_ids.astype(jnp.float32)))
    cell_len = tok_dev * col_count // grid_count
    cosines, sines = rotary_tables(cell_len, QK_HEAD)
    place = jnp.arange(cell_len, dtype=jnp.int32)
    results = []
    input_grads = []
    totals = None
    smalls = None
    for batch in range(batches):
        inputs = local_tokens[batch].astype(jnp.float32)
        norm_one, unit_one, spread_one = layer_stats_norm(inputs, pre_gain, pre_bias)
        gathered_one, projected = project_in(norm_one.astype(jnp.bfloat16), in_weight)
        query_raw = projected[:, :qk_cols].reshape(cell_len, heads_dev, QK_HEAD)
        key_raw = projected[:, qk_cols : 2 * qk_cols].reshape(cell_len, heads_dev, QK_HEAD)
        value_raw = projected[:, 2 * qk_cols : 2 * qk_cols + v_cols]
        gate_raw = projected[:, 2 * qk_cols + v_cols :]
        query_low = (query_raw * cosines + turn(query_raw) * sines).astype(jnp.bfloat16)
        key_low = (key_raw * cosines + turn(key_raw) * sines).astype(jnp.bfloat16)
        value_low = value_raw.astype(jnp.bfloat16).reshape(cell_len, heads_dev, V_HEAD)
        ends = jnp.cumsum(lengths[batch, row_index, grid_index])
        segment = jnp.sum((place[:, None] >= ends[None, :]).astype(jnp.int32), axis=1)
        mixed, states = retention_forward(query_low, key_low, value_low, segment, log_decay, CH)
        unit_out, gate_pull = jax.vjp(gate_norm, mixed, gate_raw, group_gain, group_bias)
        gathered_two, attn_out = project_out(unit_out.astype(jnp.bfloat16), output_weight)
        resid = inputs + attn_out
        norm_two, unit_two, spread_two = layer_stats_norm(resid, mid_gain, mid_bias)
        gathered_three, pre_act = project_in(norm_two.astype(jnp.bfloat16), up_weight)
        activated, gelu_pull = jax.vjp(exact_gelu, pre_act)
        gathered_four, ffn_out = project_out(activated.astype(jnp.bfloat16), down_weight)
        results.append((resid + ffn_out).astype(jnp.bfloat16))
        top_grad = local_grads[batch]
        down_part, grad_act = back_out(top_grad, down_weight, gathered_four)
        (grad_pre,) = gelu_pull(grad_act)
        up_part, grad_norm_two = back_in(grad_pre.astype(jnp.bfloat16), up_weight, gathered_three)
        resid_part, mid_gain_part, mid_bias_part = norm_back(
            grad_norm_two, unit_two, spread_two, mid_gain
        )
        grad_resid = top_grad.astype(jnp.float32) + resid_part
        out_part, grad_unit = back_out(grad_resid.astype(jnp.bfloat16), output_weight, gathered_two)
        grad_mixed, grad_gate, group_gain_part, group_bias_part = gate_pull(grad_unit)
        grad_query, grad_key, grad_value = retention_backward(
            query_low,
            key_low,
            value_low,
            segment,
            states,
            grad_mixed.astype(jnp.bfloat16),
            log_decay,
            CH,
        )
        grad_query = grad_query * cosines + turn_back(grad_query * sines)
        grad_key = grad_key * cosines + turn_back(grad_key * sines)
        grad_proj = jnp.concatenate(
            [
                grad_query.reshape(cell_len, qk_cols),
                grad_key.reshape(cell_len, qk_cols),
                grad_value.reshape(cell_len, v_cols),
                grad_gate,
            ],
            axis=1,
        ).astype(jnp.bfloat16)
        in_part, grad_norm_one = back_in(grad_proj, in_weight, gathered_one)
        input_part, pre_gain_part, pre_bias_part = norm_back(
            grad_norm_one, unit_one, spread_one, pre_gain
        )
        input_grads.append((grad_resid + input_part).astype(jnp.bfloat16))
        parts = (in_part, out_part, up_part, down_part)
        totals = (
            parts if totals is None else tuple((total + part for total, part in zip(totals, parts)))
        )
        small_parts = (
            pre_gain_part,
            pre_bias_part,
            mid_gain_part,
            mid_bias_part,
            group_gain_part,
            group_bias_part,
        )
        smalls = (
            small_parts
            if smalls is None
            else tuple((total + part for total, part in zip(smalls, small_parts)))
        )
    totals = sum_rows(totals)
    in_total, out_total, up_total, down_total = totals
    feature_len = pre_gain.shape[0]
    group_len = group_gain.shape[0]
    spread_out = (
        embed(smalls[0], grid_index, grid_count),
        embed(smalls[1], grid_index, grid_count),
        embed(smalls[2], grid_index, grid_count),
        embed(smalls[3], grid_index, grid_count),
        embed(smalls[4], col_index, col_count),
        embed(smalls[5], col_index, col_count),
    )
    summed = lax.psum(
        (spread_out[0], spread_out[1], spread_out[2], spread_out[3], spread_out[4], spread_out[5]),
        ("row", "col", "grid"),
    )
    pregain_grad = lax.dynamic_slice_in_dim(summed[0], grid_index * feature_len, feature_len)
    prebias_grad = lax.dynamic_slice_in_dim(summed[1], grid_index * feature_len, feature_len)
    midgain_grad = lax.dynamic_slice_in_dim(summed[2], grid_index * feature_len, feature_len)
    midbias_grad = lax.dynamic_slice_in_dim(summed[3], grid_index * feature_len, feature_len)
    groupgain_grad = lax.dynamic_slice_in_dim(summed[4], col_index * group_len, group_len)
    groupbias_grad = lax.dynamic_slice_in_dim(summed[5], col_index * group_len, group_len)
    result_all = jnp.stack(results)
    grad_all = jnp.stack(input_grads)
    returned = (
        lax.all_to_all(
            pick(paged(result_all), land_order), "row", split_axis=1, concat_axis=1, tiled=True
        ),
        lax.all_to_all(
            pick(paged(grad_all), land_order), "row", split_axis=1, concat_axis=1, tiled=True
        ),
    )
    block_out = pick(returned[0], send_inverse).reshape(batches, tok_dev, half_width)
    tokens_grad = pick(returned[1], send_inverse).reshape(batches, tok_dev, half_width)
    query_grad = in_total[:, :qk_cols]
    key_grad = in_total[:, qk_cols : 2 * qk_cols]
    value_grad = in_total[:, 2 * qk_cols : 2 * qk_cols + v_cols]
    gating_grad = in_total[:, 2 * qk_cols + v_cols :]
    return (
        block_out,
        tokens_grad,
        pregain_grad,
        prebias_grad,
        query_grad,
        key_grad,
        value_grad,
        gating_grad,
        groupgain_grad,
        groupbias_grad,
        out_total,
        midgain_grad,
        midbias_grad,
        up_total,
        down_total,
    )


def swap(values, axis, bit):
    count = lax.axis_size(axis)
    return lax.ppermute(values, axis, [(one, one ^ bit) for one in range(count)])


def gather_cell(own, axis=0):
    pair = jnp.concatenate([own, swap(own, "col", 2)], axis=axis)
    return jnp.concatenate([pair, swap(pair, "col", 1)], axis=axis)


def scatter_cell(part, axis=0):
    mine, other = jnp.split(part, 2, axis=axis)
    pair = mine.astype(jnp.float32) + swap(other, "col", 1).astype(jnp.float32)
    own, away = jnp.split(pair, 2, axis=axis)
    return own + swap(away.astype(jnp.bfloat16), "col", 2).astype(jnp.float32)


def after(values, done):
    return lax.optimization_barrier((values, done))[0]


def other_halves(weights, ready):
    odd = lax.axis_index("row") % 2
    pairs = [(one, one ^ 1) for one in range(lax.axis_size("row"))]
    crossed, traded, whole = [], [], []
    for place, weight in enumerate(weights):
        half = weight.shape[0] // 2
        sent = lax.dynamic_slice_in_dim(weight, odd * half, half, axis=0)
        if place > 0:
            sent = after(sent, (crossed[place - 1], ready) if place == 1 else crossed[place - 1])
        crossed.append(swap(sent, "grid", 1))
        traded.append(lax.ppermute(crossed[place], "row", pairs))
        first = jnp.where(odd == 0, crossed[place], traded[place])
        second = jnp.where(odd == 0, traded[place], crossed[place])
        whole.append(jnp.concatenate([first, second], axis=0))
    return (crossed, traded, whole)


def dot(left, right, left_axis=1, right_axis=0):
    return lax.dot_general(
        left, right, (((left_axis,), (right_axis,)), ((), ())), preferred_element_type=jnp.float32
    )


def deal_kernel(places, deal, values, *sent):
    row, col, grid = places[0], places[1], places[2]
    for step, out in enumerate(sent):
        to_row = (2 * (row // 2) + grid) ^ step
        for batch in range(values.shape[0]):
            out[batch] = values[batch, deal[batch, col, row, to_row]]


def land_kernel(places, deal, *refs):
    row, col, grid = places[0], places[1], places[2]
    *got, out = refs
    for step, values in enumerate(got):
        from_row = (2 * (row // 2) + grid) ^ step
        for batch in range(out.shape[0]):
            out[batch, deal[batch, col, row, from_row]] = values[batch]


def page_call(kernel, places, deal, values, shapes):
    smem = pl.BlockSpec(memory_space=pltpu.SMEM)
    vmem = pl.BlockSpec(memory_space=pltpu.VMEM)
    return pl.pallas_call(
        kernel,
        in_specs=[smem, smem] + [vmem] * len(values),
        out_specs=[vmem] * len(shapes),
        out_shape=[jax.ShapeDtypeStruct(shape, jnp.bfloat16) for shape in shapes],
    )(places, deal, *values)


def page_routes(back):
    rows, cols, grids = lax.axis_size("row"), lax.axis_size("col"), lax.axis_size("grid")
    routes = []
    for step in range(4):
        pairs = []
        for row in range(rows):
            for col in range(cols):
                for grid in range(grids):
                    source = (row * cols + col) * grids + grid
                    to_row = (2 * (row // 2) + grid) ^ step
                    to_col = 2 * (col % 2) + row % 2
                    target = (to_row * cols + to_col) * grids + col // 2
                    pairs.append((target, source) if back else (source, target))
        routes.append(pairs)
    return routes


def cell_norm(values, gain, bias):
    centre = jnp.mean(values, axis=1, keepdims=True)
    spread = lax.rsqrt(jnp.mean(values * values, axis=1, keepdims=True) - centre * centre + epsilon)
    normal = (values - centre) * spread
    return ((normal * gain + bias).astype(jnp.bfloat16), normal, spread)


def cell_norm_back(grad, normal, spread, gain):
    scaled = grad * gain
    first = jnp.mean(scaled, axis=1, keepdims=True)
    second = jnp.mean(scaled * normal, axis=1, keepdims=True)
    back = (scaled - first - normal * second) * spread
    return (back, jnp.sum(grad * normal, axis=0), jnp.sum(grad, axis=0))


def rotate(values, cosines, sines):
    half = values.shape[1] // 2
    low, high = values[:, :half], values[:, half:]
    return jnp.concatenate([low * cosines - high * sines, high * cosines + low * sines], axis=1)


def rotate_back(values, cosines, sines):
    half = values.shape[1] // 2
    low, high = values[:, :half], values[:, half:]
    return jnp.concatenate([low * cosines + high * sines, high * cosines - low * sines], axis=1)


def score_cell(query, keys, decay, scale):
    return (dot(query, keys, 1, 1) * scale * decay).astype(jnp.bfloat16)


def mix_cell(query, values, weights, cross, state, scale):
    scaled = (query.astype(jnp.float32) * (cross * scale)).astype(jnp.bfloat16)
    return dot(weights, values) + dot(scaled, state.astype(jnp.bfloat16))


def value_cell_back(keys, weights, keep, grad_state, grad):
    kept = (keys.astype(jnp.float32) * keep).astype(jnp.bfloat16)
    return dot(weights, grad, 0, 0) + dot(kept, grad_state.astype(jnp.bfloat16))


def score_cell_back(query, keys, values, decay, cross, keep, state, grad_state, grad, scale):
    grad_raw = (dot(grad, values, 1, 1) * decay * scale).astype(jnp.bfloat16)
    grad_added = grad_state.astype(jnp.bfloat16)
    grad_query = dot(grad_raw, keys) + dot(grad, state.astype(jnp.bfloat16), 1, 1) * (cross * scale)
    grad_keys = dot(grad_raw, query, 0, 0) + dot(values, grad_added, 1, 1) * keep
    return (grad_query, grad_keys)


def local_cells(
    tokens,
    cotangent,
    lengths,
    deal_pages,
    land_slots,
    pre_gain,
    pre_bias,
    query_weight,
    key_weight,
    value_weight,
    gate_weight,
    group_gain,
    group_bias,
    output_weight,
    mid_gain,
    mid_bias,
    up_weight,
    down_weight,
):
    row_index = lax.axis_index("row")
    col_index = lax.axis_index("col")
    grid_index = lax.axis_index("grid")
    col_count = lax.axis_size("col")
    grid_count = lax.axis_size("grid")
    batches, tok_dev, half_width = tokens.shape
    page = tok_dev // 4
    cell_len = 2 * tok_dev
    qk_cols = query_weight.shape[1]
    v_cols = value_weight.shape[1]
    heads_dev = qk_cols // QK_HEAD
    scale = QK_HEAD ** (-0.5)
    everywhere = ("row", "col", "grid")

    places = jnp.stack([row_index, col_index, grid_index])
    routes, returns = page_routes(False), page_routes(True)
    half_swap = (row_index + grid_index) % 2
    page_shape = (batches, page, half_width)

    def join_pages(got):
        pairs = []
        for place in range(2):
            one, two = got[2 * place], got[2 * place + 1]
            pairs.append(
                jnp.concatenate(
                    [jnp.where(half_swap == 0, one, two), jnp.where(half_swap == 0, two, one)], axis=2
                )
            )
        return jnp.concatenate(pairs, axis=1)

    def send_pages(chosen, step):
        return lax.ppermute(chosen, everywhere, routes[step])

    def deal_pages_of(values):
        pages = values.reshape(batches, 4, page, half_width)
        return page_call(deal_kernel, places, deal_pages, [pages], [page_shape] * 4)

    def return_pages(values):
        got = []
        for step in range(4):
            rows = values[:, (step // 2) * page : (step // 2 + 1) * page]
            first, second = rows[..., :half_width], rows[..., half_width:]
            sent = jnp.where((half_swap + step) % 2 == 0, first, second)
            got.append(lax.ppermute(sent, everywhere, returns[step]))
        pages = page_call(
            land_kernel, places, deal_pages, got, [(batches, 4, page, half_width)]
        )[0]
        return pages.reshape(batches, tok_dev, half_width)

    gains = jnp.stack([pre_gain, pre_bias, mid_gain, mid_bias])
    gains = jnp.concatenate([gains, swap(gains, "grid", 1)], axis=1)
    token_pages = deal_pages_of(tokens)
    local_tokens = join_pages([send_pages(token_pages[step], step) for step in range(4)])
    pre_gain_all, pre_bias_all, mid_gain_all, mid_bias_all = gains

    own_weights = (
        jnp.concatenate([query_weight, key_weight], axis=1),
        value_weight,
        gate_weight,
        output_weight,
        up_weight,
        down_weight,
    )
    own_weights, lengths, land_slots, cotangent = after(
        (own_weights, lengths, land_slots, cotangent), (gains, tuple(token_pages))
    )
    crossed, traded, others = other_halves(own_weights, local_tokens)
    qk_all, value_all, gate_all, output_all, up_all, down_all = [
        jnp.concatenate(pair, axis=axis)
        for *pair, axis in zip(own_weights, others, (0, 0, 0, 1, 0, 1))
    ]

    head_ids = col_index * heads_dev + jnp.arange(heads_dev, dtype=jnp.int32)
    log_decay = jnp.log1p(-jnp.exp2(-5.0 - head_ids.astype(jnp.float32)))
    rates = 10000.0 ** (-jnp.arange(QK_HEAD // 2).astype(jnp.float32) / (QK_HEAD // 2))
    x_index, core_index = col_index // 2, col_index % 2
    inner = jnp.arange(page, dtype=jnp.int32)
    order = jnp.arange(8, dtype=jnp.int32)
    groups_of = x_index ^ ((order // 2) % 2)
    sources_of = 2 * ((row_index // 2) ^ (order % 2)) + (core_index ^ (order // 4))
    slots = land_slots[:, :, row_index, :].reshape(batches, -1)
    slots = slots[:, (2 * grid_index + groups_of) * 4 + sources_of]
    positions = (tok_dev * groups_of + page * slots)[:, :, None] + inner
    positions = positions.reshape(batches, cell_len)
    runs = lengths[:, row_index, grid_index]
    slot_order = jnp.arange(runs.shape[1])
    all_ends = jnp.sum(
        jnp.where(slot_order[:, None] <= slot_order[None, :], runs[:, :, None], 0), axis=1
    )
    tables = []
    for batch in range(batches):
        position = positions[batch]
        angles = position.astype(jnp.float32)[:, None] * rates[None, :]
        ends = all_ends[batch]
        segment = jnp.sum((position[:, None] >= ends[None, :]).astype(jnp.int32), axis=1)
        last = jnp.sum((cell_len - 1 >= ends).astype(jnp.int32))
        distance = position[:, None] - position[None, :]
        same = (segment[:, None] == segment[None, :]) & (distance >= 0)
        span = jnp.maximum(distance, 0).astype(jnp.float32)
        decays = [
            jnp.where(same, jnp.exp(log_decay[head] * span), 0.0) for head in range(heads_dev)
        ]
        crosses = [
            jnp.where(
                segment == -1, jnp.exp(log_decay[head] * (position + 1).astype(jnp.float32)), 0.0
            )[:, None]
            for head in range(heads_dev)
        ]
        keeps = [
            jnp.where(
                segment == last,
                jnp.exp(log_decay[head] * (cell_len - 1 - position).astype(jnp.float32)),
                0.0,
            )[:, None]
            for head in range(heads_dev)
        ]
        tables.append((jnp.cos(angles), jnp.sin(angles), decays, crosses, keeps))
    state = jnp.zeros((QK_HEAD, V_HEAD), jnp.float32)
    grad_state = jnp.zeros((QK_HEAD, V_HEAD), jnp.float32)

    marks = [()]

    def hold(values, *others):
        return after(values, (marks[0], *others))

    def mark(*values):
        marks[0] = values

    def tall(parts):
        return jnp.concatenate(parts, axis=0)

    every = range(batches)
    head_slices = [slice(head * V_HEAD, (head + 1) * V_HEAD) for head in range(heads_dev)]
    inputs, normal_one, cell_one = [], [], []
    for batch in every:
        inputs.append(hold(local_tokens[batch], crossed[0]).astype(jnp.float32))
        hidden, unit, spread = cell_norm(inputs[batch], pre_gain_all, pre_bias_all)
        normal_one.append((unit, spread))
        mark(hidden)
        cell_one.append(gather_cell(hidden))

    scores, heads, grads_got = [], [], []
    grad_pages = list(hold(tuple(deal_pages_of(cotangent))))
    for batch in every:
        cosines, sines, decays, crosses, keeps = tables[batch]
        qk_raw = dot(hold(cell_one[batch], *crossed[1 : 1 + batch]), qk_all)
        parts = []
        for head in range(heads_dev):
            qk = slice(head * QK_HEAD, (head + 1) * QK_HEAD)
            query = rotate(qk_raw[:, qk], cosines, sines).astype(jnp.bfloat16)
            keys = rotate(qk_raw[:, qk_cols:][:, qk], cosines, sines).astype(jnp.bfloat16)
            parts.append((query, keys, score_cell(query, keys, decays[head], scale)))
        scores.append(parts)
        mark([part[2] for part in parts])
        pair = hold(tuple(grad_pages[2 * batch : 2 * batch + 2]))
        grads_got.extend(send_pages(pair[place], 2 * batch + place) for place in range(2))
    for batch in every:
        crosses = tables[batch][3]
        value_low = dot(hold(cell_one[batch], *crossed[2 : 2 + batch]), value_all).astype(jnp.bfloat16)
        kept = []
        for head, vs in enumerate(head_slices):
            query, keys, weights = scores[batch][head]
            values = value_low[:, vs]
            mixed = mix_cell(query, values, weights, crosses[head], state, scale)
            centred = mixed - jnp.mean(mixed, axis=1, keepdims=True)
            spread = lax.rsqrt(jnp.mean(centred * centred, axis=1, keepdims=True) + epsilon)
            kept.append((query, keys, values, weights, centred * spread, spread))
        heads.append(kept)
        mark([one[4] for one in kept])
    local_grads = hold(join_pages(grads_got))
    top_cells = gather_cell(local_grads, axis=1)
    top_cell = [top_cells[batch] for batch in every]
    top_tall = top_cells.reshape(-1, top_cells.shape[2])
    gates, unit_out = [], []
    for batch in every:
        gate = dot(hold(cell_one[batch], *crossed[3 : 3 + batch]), gate_all)
        gated = []
        for head, vs in enumerate(head_slices):
            scaled = heads[batch][head][4] * group_gain[vs] + group_bias[vs]
            gated.append((gate[:, vs] * jax.nn.sigmoid(gate[:, vs]) * scaled).astype(jnp.bfloat16))
        gates.append([gate[:, vs] for vs in head_slices])
        unit_out.append(jnp.concatenate(gated, axis=1))
        mark(unit_out[batch])
    attn_out = []
    for batch in every:
        part = dot(hold(unit_out[batch], *crossed[4 : 4 + batch]), output_all).astype(jnp.bfloat16)
        mark(part)
        attn_out.append(scatter_cell(part))

    resid, normal_two, cell_two = [], [], []
    for batch in every:
        resid.append(inputs[batch] + hold(attn_out[batch], crossed[5]))
        hidden, unit, spread = cell_norm(resid[batch], mid_gain_all, mid_bias_all)
        normal_two.append((unit, spread))
        mark(hidden)
        cell_two.append(gather_cell(hidden))

    activated, grad_pre, grad_two = [], [], []
    for batch in every:
        pre_act = dot(hold(cell_two[batch]), up_all)
        active, gelu_pull = jax.vjp(exact_gelu, pre_act)
        activated.append(active.astype(jnp.bfloat16))
        (grad,) = gelu_pull(dot(top_cell[batch], down_all, 1, 1))
        grad_pre.append(grad.astype(jnp.bfloat16))
        part = dot(grad_pre[batch], up_all, 1, 1).astype(jnp.bfloat16)
        mark(part, activated[batch])
        grad_two.append(scatter_cell(part))

    row_edge = (row_index == 0) | (row_index == 3)
    chunks, swapped, fresh_sums, row_sums, totals, finals = [], [], {}, {}, {}, []
    flights = []

    def chunk_dots(left, right, axis):
        made = []
        for place in range(2):
            rows = slice(place * 512, place * 512 + 512)
            if axis == 1:
                own, other = (left[:, rows], right[:, :1024]), (left[:, rows], right[:, 1024:])
            else:
                own = (left[:, rows], right)
                other = (left[:, 1024 + place * 512 : 1024 + place * 512 + 512], right)
            made.append((dot(*own, 0, 0), dot(*other, 0, 0).astype(jnp.bfloat16)))
        mark(made)
        return made

    def tick(chunk=None):
        now = len(flights)
        past = flights[-1] if flights else ()
        flying = []
        first, second, third = now - 1, now - 2, now - 3
        fresh = total = None
        if 0 <= first < len(chunks):
            fresh = (chunks[first] + swapped[first].astype(jnp.float32)).astype(jnp.bfloat16)
        if 0 <= third < len(chunks):
            total = totals[third]
        if chunk is not None:
            own, other = chunk
            swapped.append(swap(after(other, past), "grid", 1))
            chunks.append(own)
            flying.append(swapped[now])
        if 0 <= second < len(row_sums):
            other = lax.ppermute(after(row_sums[second], past), "row", [(1, 2), (2, 1)])
            flying.append(other)
            totals[second] = (
                row_sums[second].astype(jnp.float32) + other.astype(jnp.float32)
            ).astype(jnp.bfloat16)
        if fresh is not None or total is not None:
            if total is None:
                sent, pairs = fresh, [(0, 1), (3, 2)]
            elif fresh is None:
                sent, pairs = total, [(1, 0), (2, 3)]
            else:
                sent = jnp.where(row_edge, fresh, total)
                pairs = [(0, 1), (1, 0), (2, 3), (3, 2)]
            got = lax.ppermute(after(sent, past), "row", pairs)
            flying.append(got)
            if fresh is not None:
                row_sums[first] = (fresh.astype(jnp.float32) + got.astype(jnp.float32)).astype(
                    jnp.bfloat16
                )
            if total is not None:
                finals.append(jnp.where(row_edge, got, total).astype(jnp.float32))
        marks[0] = (marks[0], past)
        flights.append(tuple(flying))

    down_chunks = chunk_dots(hold(tall(activated)), top_tall, 1)
    tick(down_chunks[0])
    down_out = jnp.stack([dot(hold(one), down_all).astype(jnp.bfloat16) for one in activated])
    mark(down_out)
    ffn_out = scatter_cell(down_out, axis=1)

    grad_resid, mid_cell, mid_parts = [], [], []
    for batch in every:
        unit, spread = normal_two[batch]
        back, *small = cell_norm_back(hold(grad_two[batch]), unit, spread, mid_gain_all)
        mid_parts.append(small)
        grad_resid.append(local_grads[batch].astype(jnp.float32) + back)
        low = grad_resid[batch].astype(jnp.bfloat16)
        mark(low)
        mid_cell.append(gather_cell(low))
        if batch == 0:
            tick(down_chunks[1])
    up_chunks = chunk_dots(hold(tall(cell_two)), tall(grad_pre), 0)
    tick(up_chunks[0])
    results = (jnp.stack(resid) + hold(ffn_out)).astype(jnp.bfloat16)
    mark(results)
    block_out = return_pages(results)

    grad_mixed, grad_gate, grad_value, group_parts = [], [], [], []
    for batch in every:
        keeps = tables[batch][4]
        grad_unit = dot(hold(mid_cell[batch]), output_all, 1, 1)
        mixed_parts, gate_parts, value_parts, gain_parts, bias_parts = [], [], [], [], []
        for head, vs in enumerate(head_slices):
            query, keys, values, weights, normal, spread = heads[batch][head]
            gate_part = gates[batch][head]
            grad_u = grad_unit[:, vs]
            sig = jax.nn.sigmoid(gate_part)
            scaled = normal * group_gain[vs] + group_bias[vs]
            gate_parts.append(
                (grad_u * scaled * (sig * (1.0 + gate_part * (1.0 - sig)))).astype(jnp.bfloat16)
            )
            grad_scaled = grad_u * (gate_part * sig)
            gain_parts.append(jnp.sum(grad_scaled * normal, axis=0))
            bias_parts.append(jnp.sum(grad_scaled, axis=0))
            grad_normal = grad_scaled * group_gain[vs]
            grad = spread * (
                grad_normal
                - jnp.mean(grad_normal, axis=1, keepdims=True)
                - normal * jnp.mean(grad_normal * normal, axis=1, keepdims=True)
            )
            mixed_parts.append(grad.astype(jnp.bfloat16))
            value_parts.append(
                value_cell_back(keys, weights, keeps[head], grad_state, mixed_parts[head]).astype(
                    jnp.bfloat16
                )
            )
        grad_mixed.append(mixed_parts)
        grad_gate.append(jnp.concatenate(gate_parts, axis=1))
        grad_value.append(jnp.concatenate(value_parts, axis=1))
        group_parts.append((jnp.concatenate(gain_parts), jnp.concatenate(bias_parts)))
        mark(grad_gate[batch], grad_value[batch])
        if batch == 0:
            tick(up_chunks[1])
    out_chunks = chunk_dots(hold(tall(unit_out), block_out), tall(mid_cell), 1)
    tick(out_chunks[0])
    cells = tall(cell_one)
    gate_chunks = chunk_dots(hold(cells), tall(grad_gate), 0)
    tick(out_chunks[1])
    grad_qk = []
    for batch in every:
        cosines, sines, decays, crosses, keeps = tables[batch]
        query_parts, key_parts = [], []
        for head in range(heads_dev):
            query, keys, values, weights, normal, spread = heads[batch][head]
            grad_query, grad_keys = score_cell_back(
                query,
                keys,
                values,
                decays[head],
                crosses[head],
                keeps[head],
                state,
                grad_state,
                hold(grad_mixed[batch][head]),
                scale,
            )
            query_parts.append(rotate_back(grad_query, cosines, sines).astype(jnp.bfloat16))
            key_parts.append(rotate_back(grad_keys, cosines, sines).astype(jnp.bfloat16))
        grad_qk.append(jnp.concatenate(query_parts + key_parts, axis=1))
        mark(grad_qk[batch])
        tick(gate_chunks[batch])
    value_chunks = chunk_dots(hold(cells), tall(grad_value), 0)
    tick(value_chunks[0])
    qk_chunks = chunk_dots(hold(cells), tall(grad_qk), 0)
    tick(value_chunks[1])

    grad_one = []
    for batch in every:
        part = (
            dot(hold(grad_qk[batch]), qk_all, 1, 1)
            + dot(grad_value[batch], value_all, 1, 1)
            + dot(grad_gate[batch], gate_all, 1, 1)
        ).astype(jnp.bfloat16)
        mark(part)
        grad_one.append(scatter_cell(part))
        tick(qk_chunks[batch])
    pre_parts, input_grads = [], []
    for batch in every:
        unit, spread = normal_one[batch]
        back, *small = cell_norm_back(hold(grad_one[batch]), unit, spread, pre_gain_all)
        pre_parts.append(small)
        input_grads.append((grad_resid[batch] + back).astype(jnp.bfloat16))
        mark(input_grads[batch])
    tokens_grad = return_pages(jnp.stack(input_grads))
    for _ in range(3):
        tick()
    down_grad, up_grad, out_grad, gating_grad, value_grad = [
        jnp.concatenate(finals[place : place + 2], axis=0) for place in range(0, 10, 2)
    ]
    query_grad = jnp.concatenate([part[:, :qk_cols] for part in finals[10:]], axis=0)
    key_grad = jnp.concatenate([part[:, qk_cols:] for part in finals[10:]], axis=0)

    feature_len = pre_gain.shape[0]
    features = jnp.stack([sum(parts) for parts in (*zip(*pre_parts), *zip(*mid_parts))])
    groups = jnp.stack([sum(parts) for parts in zip(*group_parts)])
    sent = jnp.concatenate([features[:, feature_len:], groups])
    smalls = jnp.concatenate([features[:, :feature_len], groups]) + swap(sent, "grid", 1)
    smalls = smalls + swap(smalls, "row", 1)
    smalls = smalls + swap(smalls, "row", 2)
    features, groups = smalls[:4], smalls[4:]
    features = features + swap(features, "col", 1)
    features = features + swap(features, "col", 2)
    return (
        block_out,
        tokens_grad,
        features[0],
        features[1],
        query_grad,
        key_grad,
        value_grad,
        gating_grad,
        groups[0],
        groups[1],
        out_grad,
        features[2],
        features[3],
        up_grad,
        down_grad,
    )


def local(*arguments):
    tokens, query_weight = arguments[0], arguments[7]
    sizes = tuple(lax.axis_size(axis) for axis in ("row", "col", "grid"))
    one_block = 2 * tokens.shape[1] == CH
    if sizes == (4, 4, 2) and one_block and query_weight.shape[1] % QK_HEAD == 0:
        return local_cells(*arguments)
    return local_general(*arguments)


def solution(mesh):
    placed = (
        P(None, ("row", "col"), "grid"),
        P(None, ("row", "col"), "grid"),
        P(),
        P(),
        P(),
        P("grid"),
        P("grid"),
        P("grid", "col"),
        P("grid", "col"),
        P("grid", "col"),
        P("grid", "col"),
        P("col"),
        P("col"),
        P("col", "grid"),
        P("grid"),
        P("grid"),
        P("grid", "col"),
        P("col", "grid"),
    )
    return jax.shard_map(
        local,
        mesh=mesh,
        in_specs=placed,
        out_specs=(
            P(None, ("row", "col"), "grid"),
            P(None, ("row", "col"), "grid"),
            P("grid"),
            P("grid"),
            P("grid", "col"),
            P("grid", "col"),
            P("grid", "col"),
            P("grid", "col"),
            P("col"),
            P("col"),
            P("col", "grid"),
            P("grid"),
            P("grid"),
            P("grid", "col"),
            P("col", "grid"),
        ),
        check_vma=False,
    )
```
